256 devices in a mesh: grp: 8 (over x, core), seq: 32 (over y, z).
Axes of the slice: x: 4, y: 4, z: 8, core: 2. Of those that a mesh axis runs over, the one named last changes fastest.
Arguments:
- queries: bfloat16 [32768, 512], P(('grp', 'seq')), may hold values from -4.5 to 5.5
- key_vectors: bfloat16 [32768, 512], P(('grp', 'seq')), may hold values from -4.5 to 5.5
- value_vectors: bfloat16 [32768, 1024], P(('grp', 'seq')), may hold values from -6 to 6
- input_gate: float32 [4, 32768], P(None, ('grp', 'seq')), may hold values from -4 to 114
- forget_gate: float32 [4, 32768], P(None, ('grp', 'seq')), may hold values from -3 to 25
Outputs:
- hidden_states: bfloat16 [32768, 1024], P(('grp', 'seq'))
The draws below stay inside these ranges and needn't reach their ends.
All inputs are finite; a program needn't handle non-finite values.
Results may differ from the reference program's by a relative error of at most 0.028.
Values sent between devices are 32-bit elements; how exact they have to be, the bound alone decides.
A program may use at most 64 MiB of HBM per device.

```python
import jax
import jax.numpy as jnp
from jax import lax

HEAD_GROUP = 4
KEY_DIM = 128
VAL_DIM = 256
TOK_DEV = 128
TOKEN_COUNT = 32768


def draw_queries(key, part):
    seed_one = jax.random.fold_in(key, 11)
    sample = jnp.clip(jax.random.normal(seed_one, (TOKEN_COUNT, HEAD_GROUP * KEY_DIM), jnp.float32), -5.0, 5.0)
    return (sample + 0.5).astype(jnp.bfloat16)


def draw_key_vectors(key, part):
    seed_one = jax.random.fold_in(key, 23)
    sample = jnp.clip(jax.random.normal(seed_one, (TOKEN_COUNT, HEAD_GROUP * KEY_DIM), jnp.float32), -5.0, 5.0)
    return (sample + 0.5).astype(jnp.bfloat16)


def draw_input_gate(key, part):
    gate_seeds = jax.random.split(jax.random.fold_in(key, 37), 2)
    token_part = jax.random.uniform(gate_seeds[0], (HEAD_GROUP, TOKEN_COUNT), jnp.float32, -4.0, 4.0)
    segment_length = max(TOK_DEV // 4, 1)
    level_offsets = jax.random.uniform(gate_seeds[1], (HEAD_GROUP, TOKEN_COUNT // segment_length), jnp.float32, 0.0, 100.0)
    sample = token_part + jnp.repeat(level_offsets, segment_length, axis=1)
    return sample


def draw_forget_gate(key, part):
    random_seeds = jax.random.split(jax.random.fold_in(key, 53), 6)
    slow_count = HEAD_GROUP // 2
    head_order = jax.random.permutation(random_seeds[0], HEAD_GROUP)
    lagging_variant = (head_order < slow_count)[:, None]
    blocks = TOKEN_COUNT // TOK_DEV
    block_factor = jnp.repeat(jnp.exp(jax.random.uniform(random_seeds[1], (HEAD_GROUP, blocks), jnp.float32, -0.7, 0.7)), TOK_DEV, axis=1)
    token_factor = jnp.exp(jax.random.uniform(random_seeds[2], (HEAD_GROUP, TOKEN_COUNT), jnp.float32, -0.7, 0.7))
    head_factor = jnp.exp(jax.random.uniform(random_seeds[3], (HEAD_GROUP, 1), jnp.float32, -0.5, 0.5))
    fast_rate = max(0.025, 3.0 / TOK_DEV)
    forget_factor = jnp.where(lagging_variant, 0.3 / TOKEN_COUNT, fast_rate) * head_factor * block_factor * token_factor
    spike_events = lagging_variant & (jax.random.uniform(random_seeds[4], (HEAD_GROUP, TOKEN_COUNT), jnp.float32) < 4.0 / TOKEN_COUNT)
    spike_factor = jax.random.uniform(random_seeds[5], (HEAD_GROUP, TOKEN_COUNT), jnp.float32, 0.22, 0.69)
    forget_factor = jnp.where(spike_events, spike_factor, forget_factor)
    return -forget_factor - jnp.log(-jnp.expm1(-forget_factor))


def block_levels(stream_key, shape, cuts, least, largest):
    def one(axis_at, blocks):
        steps = jax.random.uniform(jax.random.fold_in(jax.random.fold_in(stream_key, 6), axis_at), (blocks,), jnp.float32, least / len(cuts), largest / len(cuts))
        return jnp.repeat(jnp.exp(steps), shape[axis_at] // blocks).reshape((-1,) + (1,) * (len(shape) - axis_at - 1))

    loudness = one(*cuts[0])
    for cut in cuts[1:]:
        loudness = loudness * one(*cut)
    return loudness


def normal_values(key, shape, scale, bound, cuts=(), held_as=jnp.bfloat16):
    level = block_levels(key, shape, cuts, -0.22, 0.18) if cuts else 1.0
    array = jax.random.normal(key, shape, jnp.float32) * scale * level
    return jnp.minimum(jnp.maximum(array, -bound), bound).astype(held_as)


def setup_inputs(seed: int = 0) -> dict:
    key_of = jax.random.split(jax.random.key(seed), 6)
    queries = draw_queries(jax.random.fold_in(key_of[5], 71), 0)
    key_vectors = draw_key_vectors(jax.random.fold_in(key_of[5], 71), 0)
    value_vectors = normal_values(key_of[2], (TOKEN_COUNT, HEAD_GROUP * VAL_DIM), 1.0, 6.0, ((0, 256),))
    input_gate = draw_input_gate(jax.random.fold_in(key_of[5], 71), 0)
    forget_gate = draw_forget_gate(jax.random.fold_in(key_of[5], 71), 0)
    return dict(queries=queries, key_vectors=key_vectors, value_vectors=value_vectors, input_gate=input_gate, forget_gate=forget_gate)


exact_precision_mode = lax.Precision.HIGHEST
floor_value = -1.0e30


def combine_states(earlier, later):
    early_matrix, early_vector, early_top, early_decay = earlier
    late_matrix, late_vector, late_top, late_decay = later
    joined = jnp.maximum(early_top + late_decay, late_top)
    early_weight = jnp.exp(early_top + late_decay - joined)
    late_weight = jnp.exp(late_top - joined)
    new_matrix = early_weight[..., None, None] * early_matrix + late_weight[..., None, None] * late_matrix
    new_vector = early_weight[..., None] * early_vector + late_weight[..., None] * late_vector
    return (new_matrix, new_vector, joined, early_decay + late_decay)


def block_step(prefix, pieces):
    query_block, key_block, value_block, in_gate, fo_gate = pieces
    length = query_block.shape[0]
    query_scaling = KEY_DIM ** -0.5
    query_widened = query_block.astype(jnp.float32).reshape(length, HEAD_GROUP, KEY_DIM).transpose(1, 0, 2)
    key_widened = key_block.astype(jnp.float32).reshape(length, HEAD_GROUP, KEY_DIM).transpose(1, 0, 2)
    value_widened = value_block.astype(jnp.float32).reshape(length, HEAD_GROUP, VAL_DIM).transpose(1, 0, 2)
    cumulative = jnp.cumsum(jax.nn.log_sigmoid(fo_gate), axis=1)
    block_decay = cumulative[:, -1]
    weight_log = block_decay[:, None] - cumulative + in_gate
    block_top = jnp.max(weight_log, axis=1)
    weight_tensor = jnp.exp(weight_log - block_top[:, None])
    memory_matrix = jnp.einsum("cdx,cdn->cxn", key_widened, weight_tensor[:, :, None] * value_widened, precision=exact_precision_mode)
    vector = jnp.einsum("hsk,hs->hk", key_widened, weight_tensor, precision=exact_precision_mode)
    local_state = (memory_matrix, vector, block_top, block_decay)
    scores = jnp.einsum("htk,hsk->hts", query_widened, key_widened, precision=exact_precision_mode) * query_scaling
    log_decay = cumulative[:, :, None] - cumulative[:, None, :] + in_gate[:, None, :]
    rows = lax.broadcasted_iota(jnp.int32, (length, length), 0)
    cols = lax.broadcasted_iota(jnp.int32, (length, length), 1)
    log_decay = jnp.where((rows >= cols)[None], log_decay, -jnp.inf)
    row_top = jnp.max(log_decay, axis=2)
    weighted = jnp.exp(log_decay - row_top[:, :, None]) * scores
    inner_den = jnp.sum(weighted, axis=2)
    weighted_bf = lax.optimization_barrier(weighted.astype(jnp.bfloat16))
    inner_num = jnp.einsum("hts,hsv->htv", weighted_bf.astype(jnp.float32), value_widened, precision=exact_precision_mode)
    previous_memory_matrix, prev_vector, prev_top, prev_decay = prefix
    stab = jnp.maximum(cumulative + prev_top[:, None], row_top)
    inner_factor = jnp.exp(row_top - stab)
    outer_factor = jnp.exp(cumulative + prev_top[:, None] - stab)
    carried_numerator = jnp.einsum("cps,csz->cpz", query_widened, previous_memory_matrix, precision=exact_precision_mode) * query_scaling
    carried_den = jnp.einsum("htk,hk->ht", query_widened, prev_vector, precision=exact_precision_mode) * query_scaling
    numer = inner_factor[:, :, None] * inner_num + outer_factor[:, :, None] * carried_numerator
    denom = inner_factor * inner_den + outer_factor * carried_den
    output = numer / jnp.maximum(jnp.abs(denom), jnp.exp(-stab))[:, :, None]
    output = output.transpose(1, 0, 2).reshape(length, HEAD_GROUP * VAL_DIM).astype(jnp.bfloat16)
    return combine_states(prefix, local_state), output


def reference(queries, key_vectors, value_vectors, input_gate, forget_gate):
    blocks = TOKEN_COUNT // TOK_DEV
    query_blocks = queries.reshape(blocks, TOK_DEV, HEAD_GROUP * KEY_DIM)
    key_blocks = key_vectors.reshape(blocks, TOK_DEV, HEAD_GROUP * KEY_DIM)
    value_blocks = value_vectors.reshape(blocks, TOK_DEV, HEAD_GROUP * VAL_DIM)
    in_blocks = input_gate.reshape(HEAD_GROUP, blocks, TOK_DEV).transpose(1, 0, 2)
    fo_blocks = forget_gate.reshape(HEAD_GROUP, blocks, TOK_DEV).transpose(1, 0, 2)
    start = (jnp.zeros((HEAD_GROUP, KEY_DIM, VAL_DIM), jnp.float32), jnp.zeros((HEAD_GROUP, KEY_DIM), jnp.float32),
             jnp.full((HEAD_GROUP,), floor_value, jnp.float32), jnp.zeros((HEAD_GROUP,), jnp.float32))
    final_state, outputs = lax.scan(block_step, start, (query_blocks, key_blocks, value_blocks, in_blocks, fo_blocks))
    return outputs.reshape(TOKEN_COUNT, HEAD_GROUP * VAL_DIM)
```

```python
import functools

import jax
import jax.numpy as jnp
from jax import lax
from jax.experimental import pallas as pl
from jax.experimental.pallas import tpu as pltpu
from jax.sharding import PartitionSpec as P

MESH = pl.DeviceIdType.MESH
FLOOR = -1e30
CHUNKS = 1
EXACT = lax.Precision.HIGHEST


def split3(x):
    hi = x.astype(jnp.bfloat16)
    rest = x - hi.astype(jnp.float32)
    mid = rest.astype(jnp.bfloat16)
    low = (rest - mid.astype(jnp.float32)).astype(jnp.bfloat16)
    return hi, mid, low


def kernel(
    ng, ns, heads, kd, vd, length,
    q_hbm, k_hbm, v_hbm, ig_ref, fg_ref, o_ref,
    qv, kv, vv, state, inner, rbuf, pbuf, pfull, scal, rscal, gsend, grecv, gscal, grscal,
    acoef, bcoef, tops, decs, nbuf,
    in_sem, s1, r1, ss, rs, sg, rg, sgs, rgs, s3, r3,
):
    hc = heads // CHUNKS
    rp = kd * (vd // 128) // ns
    cols = vd // 128
    scale = kd ** (-0.5)
    myg = lax.axis_index("grp")
    me = lax.axis_index("seq")

    def seq_peer(d):
        return lax.rem(me + d, ns)

    def grp_peer(d):
        return lax.rem(myg + d, ng)

    copies = [
        pltpu.make_async_copy(src, dst, in_sem.at[n])
        for n, (src, dst) in enumerate(((k_hbm, kv), (v_hbm, vv), (q_hbm, qv)))
    ]
    for copy in copies:
        copy.start()

    barrier = pltpu.get_barrier_semaphore()

    @pl.loop(1, ns)
    def _(d):
        pl.semaphore_signal(barrier, inc=1, device_id=(myg, seq_peer(d)), device_id_type=MESH)

    @pl.loop(1, ng)
    def _(d):
        pl.semaphore_signal(barrier, inc=1, device_id=(grp_peer(d), me), device_id_type=MESH)

    lane = lax.broadcasted_iota(jnp.int32, (heads, 128), 1)
    rows = lax.broadcasted_iota(jnp.int32, (length, length), 0)
    lanes = lax.broadcasted_iota(jnp.int32, (length, length), 1)

    def pack(left, right):
        return jnp.where(lane < 64, left, right)

    def unpack(row):
        turned = pltpu.roll(row, 64, 1)
        return jnp.where(lane < 64, row, turned), jnp.where(lane < 64, turned, row)

    forget = fg_ref[...]
    gate = ig_ref[...]
    logf = jnp.minimum(forget, 0.0) - jnp.log1p(jnp.exp(-jnp.abs(forget)))
    upper = jnp.where(rows <= lanes, 1.0, 0.0)
    cumul = jnp.dot(logf, upper, precision=EXACT, preferred_element_type=jnp.float32)
    decay = jnp.sum(jnp.where(lane == length - 1, cumul, 0.0), axis=1, keepdims=True)
    level = gate - cumul
    wlog = decay + level
    top = jnp.max(wlog, axis=1, keepdims=True)
    weight = jnp.exp(wlog - top)
    decay_row = jnp.broadcast_to(decay, (heads, 128))
    top_row = jnp.broadcast_to(top, (heads, 128))

    copies[0].wait()
    hi, mid, low = split3(weight)
    lhs = jnp.concatenate([hi, mid, low, jnp.zeros_like(low)], axis=0)
    for h in range(heads):
        part = jnp.dot(lhs, kv[:, h * kd : (h + 1) * kd], preferred_element_type=jnp.float32)
        scal[h : h + 1, :] = (
            part[h : h + 1] + part[heads + h : heads + h + 1] + part[2 * heads + h : 2 * heads + h + 1]
        )
    scal[heads : 2 * heads, :] = pack(decay_row, top_row)
    rscal[me] = scal[...]

    pl.semaphore_wait(barrier, ns - 1 + ng - 1)

    def scal_copy(d):
        return pltpu.make_async_remote_copy(
            src_ref=scal, dst_ref=rscal.at[me], send_sem=ss.at[d], recv_sem=rs.at[me],
            device_id=(myg, seq_peer(d)), device_id_type=MESH,
        )

    @pl.loop(1, ns)
    def _(d):
        scal_copy(d).start()

    copies[1].wait()

    def slice_of(ref, c, o):
        row = pl.multiple_of(lax.div(o, cols) * rp, 8)
        col = pl.multiple_of(lax.rem(o, cols) * 128, 128)
        return ref.at[pl.ds(c * hc, hc), pl.ds(row, rp), pl.ds(col, 128)]

    def state_copy(c, d):
        o = seq_peer(d)
        return pltpu.make_async_remote_copy(
            src_ref=slice_of(state, c, o), dst_ref=rbuf.at[me, pl.ds(c * hc, hc)],
            send_sem=s1.at[c, d], recv_sem=r1.at[c, me], device_id=(myg, o), device_id_type=MESH,
        )

    for c in range(CHUNKS):
        for h in range(c * hc, (c + 1) * hc):
            turned = kv[:, h * kd : (h + 1) * kd].astype(jnp.float32).T
            scaled = (turned * weight[h : h + 1, :]).astype(jnp.bfloat16)
            state[h] = jnp.dot(
                scaled, vv[:, h * vd : (h + 1) * vd], preferred_element_type=jnp.float32
            )

        @pl.loop(1, ns)
        def _(d, c=c):
            state_copy(c, d).start()

        rbuf[me, c * hc : (c + 1) * hc] = slice_of(state, c, me)[...]

    copies[2].wait()
    columns = []
    for h in range(heads):
        scores = scale * lax.dot_general(
            qv[:, h * kd : (h + 1) * kd], kv[:, h * kd : (h + 1) * kd],
            (((1,), (1,)), ((), ())), preferred_element_type=jnp.float32,
        )
        masked = jnp.where(rows >= lanes, level[h : h + 1, :], -jnp.inf)
        reach = jnp.max(masked, axis=1, keepdims=True)
        weighted = jnp.exp(masked - reach) * scores
        inner_den = jnp.sum(weighted, axis=1, keepdims=True)
        cumul_col = jnp.sum(
            jnp.where(rows == lanes, cumul[h : h + 1, :], 0.0), axis=1, keepdims=True
        )
        inner[h] = jnp.dot(
            weighted.astype(jnp.bfloat16), vv[:, h * vd : (h + 1) * vd],
            preferred_element_type=jnp.float32,
        )
        columns.append((reach, inner_den, cumul_col))

    @pl.loop(1, ns)
    def _(d):
        src = seq_peer(d)
        pltpu.make_async_remote_copy(
            src_ref=scal, dst_ref=rscal.at[src], send_sem=ss.at[d], recv_sem=rs.at[src],
            device_id=(myg, src), device_id_type=MESH,
        ).wait_recv()

    run_top = jnp.full((heads, 128), FLOOR, jnp.float32)
    run_dec = jnp.zeros((heads, 128), jnp.float32)
    run_vec = jnp.zeros((heads, 128), jnp.float32)
    for i in range(ns):
        dec_i, top_i = unpack(rscal[i, heads : 2 * heads, :])
        tops[i] = run_top
        decs[i] = run_dec
        nbuf[i] = run_vec
        early = run_top + dec_i
        joined = jnp.maximum(early, top_i)
        a = jnp.exp(early - joined)
        b = jnp.exp(top_i - joined)
        acoef[i] = a
        bcoef[i] = b
        run_vec = a * run_vec + b * rscal[i, 0:heads, :]
        run_top = joined
        run_dec = run_dec + dec_i
    gscal[0:heads, :] = run_vec
    gscal[heads : 2 * heads, :] = pack(run_dec, run_top)
    grscal[myg] = gscal[...]

    @pl.loop(1, ng)
    def _(d):
        pltpu.make_async_remote_copy(
            src_ref=gscal, dst_ref=grscal.at[myg], send_sem=sgs.at[d], recv_sem=rgs.at[myg],
            device_id=(grp_peer(d), me), device_id_type=MESH,
        ).start()

    for c in range(CHUNKS):
        @pl.loop(1, ns)
        def _(d, c=c):
            src = seq_peer(d)
            pltpu.make_async_remote_copy(
                src_ref=slice_of(state, c, src), dst_ref=rbuf.at[src, pl.ds(c * hc, hc)],
                send_sem=s1.at[c, d], recv_sem=r1.at[c, src], device_id=(myg, src), device_id_type=MESH,
            ).wait_recv()

        for h in range(c * hc, (c + 1) * hc):
            run = jnp.zeros((rp, 128), jnp.float32)
            for i in range(ns):
                pbuf[i, h] = run
                run = acoef[i, h : h + 1, :] * run + bcoef[i, h : h + 1, :] * rbuf[i, h]
            gsend[h] = run
        grecv[myg, c * hc : (c + 1) * hc] = gsend[c * hc : (c + 1) * hc]

        @pl.loop(1, ng)
        def _(d, c=c):
            pltpu.make_async_remote_copy(
                src_ref=gsend.at[pl.ds(c * hc, hc)], dst_ref=grecv.at[myg, pl.ds(c * hc, hc)],
                send_sem=sg.at[c, d], recv_sem=rg.at[c, myg], device_id=(grp_peer(d), me), device_id_type=MESH,
            ).start()

    @pl.loop(1, ng)
    def _(d):
        src = grp_peer(d)
        pltpu.make_async_remote_copy(
            src_ref=gscal, dst_ref=grscal.at[src], send_sem=sgs.at[d], recv_sem=rgs.at[src],
            device_id=(src, me), device_id_type=MESH,
        ).wait_recv()

    before_top = jnp.full((heads, 128), FLOOR, jnp.float32)
    before_vec = jnp.zeros((heads, 128), jnp.float32)
    weights = []
    for g in range(ng):
        dec_g, top_g = unpack(grscal[g, heads : 2 * heads, :])
        counts = g < myg
        early = before_top + dec_g
        joined = jnp.maximum(early, top_g)
        a = jnp.where(counts, jnp.exp(early - joined), 1.0)
        b = jnp.where(counts, jnp.exp(top_g - joined), 0.0)
        before_vec = a * before_vec + b * grscal[g, 0:heads, :]
        before_top = jnp.where(counts, joined, before_top)
        weights.append((a, b))

    for i in range(ns):
        early = before_top + decs[i]
        full = jnp.maximum(early, tops[i])
        acoef[i] = jnp.exp(early - full)
        bcoef[i] = jnp.exp(tops[i] - full)
        tops[i] = full
    prev_top = tops[me]
    prev_vec = acoef[me] * before_vec + bcoef[me] * nbuf[me]

    def back_copy(c, d, src):
        o = seq_peer(d)
        return pltpu.make_async_remote_copy(
            src_ref=pbuf.at[o, pl.ds(c * hc, hc)], dst_ref=slice_of(pfull, c, src),
            send_sem=s3.at[c, d], recv_sem=r3.at[c, src], device_id=(myg, o), device_id_type=MESH,
        )

    for c in range(CHUNKS):
        @pl.loop(1, ng)
        def _(d, c=c):
            src = grp_peer(d)
            pltpu.make_async_remote_copy(
                src_ref=gsend.at[pl.ds(c * hc, hc)], dst_ref=grecv.at[src, pl.ds(c * hc, hc)],
                send_sem=sg.at[c, d], recv_sem=rg.at[c, src], device_id=(src, me), device_id_type=MESH,
            ).wait_recv()

        for h in range(c * hc, (c + 1) * hc):
            run = jnp.zeros((rp, 128), jnp.float32)
            for g in range(ng):
                a, b = weights[g]
                run = a[h : h + 1, :] * run + b[h : h + 1, :] * grecv[g, h]
            for i in range(ns):
                pbuf[i, h] = acoef[i, h : h + 1, :] * run + bcoef[i, h : h + 1, :] * pbuf[i, h]

        @pl.loop(1, ns)
        def _(d, c=c):
            back_copy(c, d, me).start()

        slice_of(pfull, c, me)[...] = pbuf[me, c * hc : (c + 1) * hc]

    for c in range(CHUNKS):
        @pl.loop(1, ns)
        def _(d, c=c):
            back_copy(c, d, seq_peer(d)).wait_recv()

        for h in range(c * hc, (c + 1) * hc):
            reach, inner_den, cumul_col = columns[h]
            query = qv[:, h * kd : (h + 1) * kd]
            carried = scale * jnp.dot(
                query, pfull[h].astype(jnp.bfloat16), preferred_element_type=jnp.float32
            )
            carried_den = scale * jnp.sum(
                query.astype(jnp.float32) * prev_vec[h : h + 1, :], axis=1, keepdims=True
            )
            prev = jnp.max(prev_top[h : h + 1, :], axis=1, keepdims=True)
            peak = jnp.maximum(prev, reach)
            inner_factor = jnp.exp(reach - peak)
            outer_factor = jnp.exp(prev - peak)
            denom = inner_factor * inner_den + outer_factor * carried_den
            bound = jnp.maximum(jnp.abs(denom), jnp.exp(-(cumul_col + peak)))
            numer = inner_factor * inner[h] + outer_factor * carried
            o_ref[:, h * vd : (h + 1) * vd] = (numer / bound).astype(jnp.bfloat16)

    @pl.loop(1, ns)
    def _(d):
        scal_copy(d).wait_send()
        for c in range(CHUNKS):
            state_copy(c, d).wait_send()
            back_copy(c, d, me).wait_send()

    @pl.loop(1, ng)
    def _(d):
        pltpu.make_async_remote_copy(
            src_ref=gscal, dst_ref=grscal.at[myg], send_sem=sgs.at[d], recv_sem=rgs.at[myg],
            device_id=(grp_peer(d), me), device_id_type=MESH,
        ).wait_send()
        for c in range(CHUNKS):
            pltpu.make_async_remote_copy(
                src_ref=gsend.at[pl.ds(c * hc, hc)], dst_ref=grecv.at[myg, pl.ds(c * hc, hc)],
                send_sem=sg.at[c, d], recv_sem=rg.at[c, myg], device_id=(grp_peer(d), me), device_id_type=MESH,
            ).wait_send()


def on_device(ng, ns, queries, key_vectors, value_vectors, input_gate, forget_gate):
    heads, length = input_gate.shape
    kd = queries.shape[1] // heads
    vd = value_vectors.shape[1] // heads
    rp = kd * (vd // 128) // ns
    f32 = jnp.float32
    dma = pltpu.SemaphoreType.DMA
    vmem = pl.BlockSpec(memory_space=pltpu.VMEM)
    hbm = pl.BlockSpec(memory_space=pl.ANY)
    return pl.pallas_call(
        functools.partial(kernel, ng, ns, heads, kd, vd, length),
        out_shape=jax.ShapeDtypeStruct(value_vectors.shape, jnp.bfloat16),
        in_specs=[hbm, hbm, hbm, vmem, vmem],
        out_specs=vmem,
        scratch_shapes=[
            pltpu.VMEM(queries.shape, jnp.bfloat16),
            pltpu.VMEM(key_vectors.shape, jnp.bfloat16),
            pltpu.VMEM(value_vectors.shape, jnp.bfloat16),
            pltpu.VMEM((heads, kd, vd), f32),
            pltpu.VMEM((heads, length, vd), f32),
            pltpu.VMEM((ns, heads, rp, 128), f32),
            pltpu.VMEM((ns, heads, rp, 128), f32),
            pltpu.VMEM((heads, kd, vd), f32),
            pltpu.VMEM((2 * heads, 128), f32),
            pltpu.VMEM((ns, 2 * heads, 128), f32),
            pltpu.VMEM((heads, rp, 128), f32),
            pltpu.VMEM((ng, heads, rp, 128), f32),
            pltpu.VMEM((2 * heads, 128), f32),
            pltpu.VMEM((ng, 2 * heads, 128), f32),
            pltpu.VMEM((ns, heads, 128), f32),
            pltpu.VMEM((ns, heads, 128), f32),
            pltpu.VMEM((ns, heads, 128), f32),
            pltpu.VMEM((ns, heads, 128), f32),
            pltpu.VMEM((ns, heads, 128), f32),
            dma((3,)),
            dma((CHUNKS, ns)), dma((CHUNKS, ns)),
            dma((ns,)), dma((ns,)),
            dma((CHUNKS, ng)), dma((CHUNKS, ng)),
            dma((ng,)), dma((ng,)),
            dma((CHUNKS, ns)), dma((CHUNKS, ns)),
        ],
        compiler_params=pltpu.CompilerParams(collective_id=0, has_side_effects=True),
        name="mlstm_layer",
    )(queries, key_vectors, value_vectors, input_gate, forget_gate)


def solution(mesh):
    return jax.shard_map(
        functools.partial(on_device, mesh.shape["grp"], mesh.shape["seq"]),
        mesh=mesh,
        in_specs=(
            P(("grp", "seq"), None),
            P(("grp", "seq"), None),
            P(("grp", "seq"), None),
            P(None, ("grp", "seq")),
            P(None, ("grp", "seq")),
        ),
        out_specs=P(("grp", "seq"), None),
        check_vma=False,
    )
```

```python
import functools

import jax
import jax.numpy as jnp
from jax import lax
from jax.experimental import pallas as pl
from jax.experimental.pallas import tpu as pltpu
from jax.sharding import PartitionSpec as P

MESH = pl.DeviceIdType.MESH
FLOOR = -1e30
CHUNKS = 2
BACK = 1
ORDER = 1
UP = 1
EARLY = 1


def split3(x):
    hi = x.astype(jnp.bfloat16)
    rest = x - hi.astype(jnp.float32)
    mid = rest.astype(jnp.bfloat16)
    low = (rest - mid.astype(jnp.float32)).astype(jnp.bfloat16)
    return hi, mid, low


def kernel(
    ng, ns, heads, kd, vd, length,
    q_hbm, k_hbm, v_hbm, ig_hbm, fg_hbm, o_ref,
    ig, fg, qv, kv, vv, state, inner, rbuf, pbuf, pfull, gsend, grecv,
    small, rsmall, gsmall, grsmall, vec, rvec, gvec, grvec, nback, rnback, nrows,
    rows_a, rows_b, rows_t, rows_d, wide_a, wide_b, wide_c, wide_d, group_a, group_b, group_wide_a, group_wide_b,
    in_sem, s1, r1, ss, rs, sg, rg, sgs, rgs, s3, r3, sn, rn, sv, rv, sgv, rgv,
):
    f32, bf16 = jnp.float32, jnp.bfloat16
    hc = heads // CHUNKS
    rp = kd * (vd // 128) // ns
    cols = vd // 128
    ydim = max(1, ns // 8)
    zdim = ns // ydim
    per_head = ns // heads
    span = 64 // heads
    scale = kd ** (-0.5)
    myg = lax.axis_index("grp")
    me = lax.axis_index("seq")
    myh = lax.div(me, per_head)
    owns_vector = lax.rem(me, per_head) == 0

    def seq_peer(d):
        return lax.rem(me + d, ns)

    def grp_peer(d):
        return lax.rem(myg + d, ng)

    copies = [
        pltpu.make_async_copy(src, dst, in_sem.at[n])
        for n, (src, dst) in enumerate(
            ((fg_hbm, fg), (ig_hbm, ig), (k_hbm, kv), (v_hbm, vv), (q_hbm, qv))
        )
    ]
    for copy in copies:
        copy.start()

    barrier = pltpu.get_barrier_semaphore()
    zero = jnp.zeros((1, 128), f32)
    if UP:
        for g in range(ng):
            grsmall[g] = zero
            grvec[g] = zero
            for h in range(heads):
                grecv[g, h] = jnp.zeros((rp, 128), f32)

    @pl.loop(1, ns)
    def _(d):
        pl.semaphore_signal(barrier, inc=1, device_id=(myg, seq_peer(d)), device_id_type=MESH)

    @pl.loop(1, ng)
    def _(d):
        pl.semaphore_signal(barrier, inc=1, device_id=(grp_peer(d), me), device_id_type=MESH)

    lane = lax.broadcasted_iota(jnp.int32, (heads, 128), 1)
    head_row = lax.broadcasted_iota(jnp.int32, (heads, 128), 0)
    rows = lax.broadcasted_iota(jnp.int32, (length, length), 0)
    lanes = lax.broadcasted_iota(jnp.int32, (length, length), 1)

    def slice_of(ref, c, o):
        row = pl.multiple_of(lax.div(o, cols) * rp, 8)
        col = pl.multiple_of(lax.rem(o, cols) * 128, 128)
        return ref.at[pl.ds(c * hc, hc), pl.ds(row, rp), pl.ds(col, 128)]

    def part(c):
        return pl.ds(c * hc, hc)

    def remote(src, dst, send, recv, device):
        return pltpu.make_async_remote_copy(
            src_ref=src, dst_ref=dst, send_sem=send, recv_sem=recv, device_id=device, device_id_type=MESH
        )

    def small_copy(o, slot):
        return remote(
            small, rsmall.at[slot], ss.at[o], rs.at[slot], (myg, o)
        )

    def block_vector_copy(h, o, slot):
        return remote(vec.at[h], rvec.at[slot], sv.at[h], rv.at[slot], (myg, o))

    def group_vector_copy(o, slot):
        return remote(gvec, grvec.at[slot], sgv.at[o], rgv.at[slot], (o, me))

    def state_copy(c, o, slot):
        return remote(
            slice_of(state, c, o), rbuf.at[slot, part(c)], s1.at[c, o], r1.at[c, slot], (myg, o)
        )

    def back_copy(c, o, slot):
        return remote(
            pbuf.at[o, part(c)], slice_of(pfull, c, slot), s3.at[c, o], r3.at[c, slot], (myg, o)
        )

    def vector_copy(o, h):
        return remote(nback.at[o], rnback.at[h], sn.at[o], rn.at[h], (myg, o))

    def group_small_copy(o, slot):
        return remote(gsmall, grsmall.at[slot], sgs.at[o], rgs.at[slot], (o, me))

    def group_copy(c, o, slot):
        return remote(
            gsend.at[part(c)], grecv.at[slot, part(c)], sg.at[c, o], rg.at[c, slot], (o, me)
        )

    upper = jnp.where(rows <= lanes, 1.0, 0.0).astype(bf16)
    copies[0].wait()
    copies[1].wait()
    forget = fg[...]
    logf = jnp.minimum(forget, 0.0) - jnp.log1p(jnp.exp(-jnp.abs(forget)))

    def exact_rows(values, matrix):
        hi, mid, low = split3(values)
        lhs = jnp.concatenate([hi, mid, low, jnp.zeros_like(low)], axis=0)
        out = jnp.dot(lhs, matrix, preferred_element_type=f32)
        n = values.shape[0]
        return out[0:n] + out[n : 2 * n] + out[2 * n : 3 * n]

    cumul = exact_rows(logf, upper)
    level = ig[...] - cumul
    decay = cumul[:, length - 1 : length]
    level_top = jnp.max(level, axis=1, keepdims=True)
    weight = jnp.exp(level - level_top)
    top = decay + level_top

    mine = jnp.where(lane < 64, decay, top)
    pick = lax.div(lax.rem(lane, 64), span) == head_row
    scalars = jnp.sum(jnp.where(pick, mine, 0.0), axis=0, keepdims=True)

    copies[2].wait()
    copies[3].wait()

    def local_state(c):
        for h in range(c * hc, (c + 1) * hc):
            turned = kv[:, h * kd : (h + 1) * kd].astype(f32).T
            scaled = (turned * weight[h : h + 1, :]).astype(bf16)
            state[h] = jnp.dot(scaled, vv[:, h * vd : (h + 1) * vd], preferred_element_type=f32)
        rbuf[me, c * hc : (c + 1) * hc] = slice_of(state, c, me)[...]

    def send_state(c):
        @pl.loop(1, ns)
        def _(d):
            state_copy(c, seq_peer(d), me).start()

    small[...] = scalars
    rsmall[me] = scalars
    local_state(0)
    pl.semaphore_wait(barrier, ns - 1 + ng - 1)

    @pl.loop(1, ns)
    def _(d):
        small_copy(seq_peer(d), me).start()

    send_state(0)
    for c in range(1, CHUNKS):
        local_state(c)
        send_state(c)

    for h in range(heads):
        vector = exact_rows(weight, kv[:, h * kd : (h + 1) * kd])
        vec[h] = vector[h : h + 1, :]
    for h in range(heads):
        @pl.when(me == h * per_head)
        def _(h=h):
            rvec[me] = vec[h]

        @pl.when(me != h * per_head)
        def _(h=h):
            block_vector_copy(h, h * per_head, me).start()

    copies[4].wait()
    columns = []
    for h in range(heads):
        scores = scale * lax.dot_general(
            qv[:, h * kd : (h + 1) * kd], kv[:, h * kd : (h + 1) * kd],
            (((1,), (1,)), ((), ())), preferred_element_type=f32,
        )
        masked = jnp.where(rows >= lanes, level[h : h + 1, :], -jnp.inf)
        reach = jnp.max(masked, axis=1, keepdims=True)
        weighted = jnp.exp(masked - reach) * scores
        inner_den = jnp.sum(weighted, axis=1, keepdims=True)
        cumul_col = jnp.sum(
            jnp.where(rows == lanes, cumul[h : h + 1, :], 0.0), axis=1, keepdims=True
        )
        inner[h] = jnp.dot(
            weighted.astype(bf16), vv[:, h * vd : (h + 1) * vd], preferred_element_type=f32
        )
        columns.append((reach, inner_den, cumul_col))

    @pl.loop(1, ns)
    def _(d):
        o = seq_peer(d)
        small_copy(o, o).wait_recv()

    def widen(out, source):
        for h in range(heads):
            out[h] = jnp.broadcast_to(source[:, h * span : h * span + 1], (ns, 128))

    run_top = jnp.full((1, 128), FLOOR, f32)
    run_dec = jnp.zeros((1, 128), f32)
    for i in range(ns):
        row = rsmall[i]
        top_i = pltpu.roll(row, 64, 1)
        rows_t[i : i + 1, :] = run_top
        rows_d[i : i + 1, :] = run_dec
        early = run_top + row
        joined = jnp.maximum(early, top_i)
        rows_a[i : i + 1, :] = early - joined
        rows_b[i : i + 1, :] = top_i - joined
        run_top = joined
        run_dec = run_dec + row
    lane1 = lax.broadcasted_iota(jnp.int32, (1, 128), 1)
    widen(wide_a, jnp.exp(rows_a[...]))
    widen(wide_b, jnp.exp(rows_b[...]))

    total = jnp.where(lane1 < 64, run_dec, pltpu.roll(run_top, 64, 1))
    gsmall[...] = total
    grsmall[myg] = total

    @pl.loop(myg + 1 if UP else 1, ng)
    def _(d):
        group_small_copy(d if UP else grp_peer(d), myg).start()

    def scan_vector():
        @pl.when(owns_vector)
        def _():
            @pl.loop(1, ns)
            def _(d):
                o = seq_peer(d)
                block_vector_copy(0, o, o).wait_recv()

            run_vec = jnp.zeros((1, 128), f32)
            for i in range(ns):
                nrows[i : i + 1, :] = run_vec
                run_vec = wide_a[myh, i : i + 1, :] * run_vec + wide_b[myh, i : i + 1, :] * rvec[i]
            gvec[...] = run_vec
            grvec[myg] = run_vec

            @pl.loop(myg + 1 if UP else 1, ng)
            def _(d):
                group_vector_copy(d if UP else grp_peer(d), myg).start()

    def scan(c):
        @pl.loop(1, ns)
        def _(d):
            o = seq_peer(d)
            state_copy(c, o, o).wait_recv()

        for h in range(c * hc, (c + 1) * hc):
            run = jnp.zeros((rp, 128), f32)
            for i in range(ns):
                pbuf[i, h] = run
                run = wide_a[h, i : i + 1, :] * run + wide_b[h, i : i + 1, :] * rbuf[i, h]
            gsend[h] = run
        grecv[myg, c * hc : (c + 1) * hc] = gsend[c * hc : (c + 1) * hc]

        @pl.loop(myg + 1 if UP else 1, ng)
        def _(d):
            group_copy(c, d if UP else grp_peer(d), myg).start()

    if ORDER == 0:
        order = [("scan", c) for c in range(CHUNKS)] + [("back", c) for c in range(CHUNKS)]
    else:
        order = [(what, c) for c in range(CHUNKS) for what in ("scan", "back")]
    order = order[:1] + [("group", 0)] + order[1:-1] + [("vector", 0)] + order[-1:] + [("return", 0)]

    found = []

    def before_group():
        @pl.loop(0 if UP else 1, myg if UP else ng)
        def _(d):
            o = d if UP else grp_peer(d)
            group_small_copy(o, o).wait_recv()

        before_top = jnp.full((1, 128), FLOOR, f32)
        for g in range(ng):
            row = grsmall[g]
            top_g = pltpu.roll(row, 64, 1)
            counts = g < myg
            early = before_top + row
            joined = jnp.maximum(early, top_g)
            a = jnp.where(counts, jnp.exp(early - joined), 1.0)
            b = jnp.where(counts, jnp.exp(top_g - joined), 0.0)
            before_top = jnp.where(counts, joined, before_top)
            group_a[g : g + 1, :] = a
            group_b[g : g + 1, :] = b
        tops = rows_t[...]
        early = before_top + rows_d[...]
        full = jnp.maximum(early, tops)
        rows_t[...] = full
        found.append(rows_t[pl.ds(me, 1), :])
        widen(wide_c, jnp.exp(early - full))
        widen(wide_d, jnp.exp(tops - full))
        for h in range(heads):
            group_wide_a[h] = jnp.broadcast_to(group_a[:, h * span : h * span + 1], (ng, 128))
            group_wide_b[h] = jnp.broadcast_to(group_b[:, h * span : h * span + 1], (ng, 128))

    def return_vector():
        @pl.when(owns_vector)
        def _():
            @pl.loop(0 if UP else 1, myg if UP else ng)
            def _(d):
                o = d if UP else grp_peer(d)
                group_vector_copy(o, o).wait_recv()

            before = jnp.zeros((1, 128), f32)
            for g in range(ng):
                before = (
                    group_wide_a[myh, g : g + 1, :] * before
                    + group_wide_b[myh, g : g + 1, :] * grvec[g]
                )
            vectors = wide_c[myh] * before + wide_d[myh] * nrows[...]
            for i in range(ns):
                nback[i] = vectors[i : i + 1, :]
            rnback[myh] = nback[me]

            @pl.loop(1, ns)
            def _(d):
                vector_copy(seq_peer(d), myh).start()

    def back(c):
        @pl.loop(0 if UP else 1, myg if UP else ng)
        def _(d):
            o = d if UP else grp_peer(d)
            group_copy(c, o, o).wait_recv()

        for h in range(c * hc, (c + 1) * hc):
            run = jnp.zeros((rp, 128), f32)
            for g in range(ng):
                run = group_wide_a[h, g : g + 1, :] * run + group_wide_b[h, g : g + 1, :] * grecv[g, h]
            for i in range(ns):
                pbuf[i, h] = wide_c[h, i : i + 1, :] * run + wide_d[h, i : i + 1, :] * pbuf[i, h]

        if BACK == 0:
            @pl.loop(1, ns)
            def _(d):
                back_copy(c, seq_peer(d), me).start()
        else:
            z = lax.rem(me, zdim)

            @pl.loop(0, ns)
            def _(d):
                o = lax.div(d, zdim) * zdim + lax.rem(z + lax.rem(d, zdim), zdim)

                @pl.when(o != me)
                def _():
                    back_copy(c, o, me).start()
        slice_of(pfull, c, me)[...] = pbuf[me, c * hc : (c + 1) * hc]

    for what, c in order:
        if what == "scan":
            scan(c)
        elif what == "back":
            back(c)
        elif what == "group":
            before_group()
        elif what == "vector":
            scan_vector()
        else:
            return_vector()

    for h in range(heads):
        @pl.when(me != h * per_head)
        def _(h=h):
            vector_copy(h * per_head, h).wait_recv()

    for c in range(CHUNKS):
        @pl.loop(1, ns)
        def _(d, c=c):
            o = seq_peer(d)
            back_copy(c, o, o).wait_recv()

        for h in range(c * hc, (c + 1) * hc):
            reach, inner_den, cumul_col = columns[h]
            query = qv[:, h * kd : (h + 1) * kd]
            carried = scale * jnp.dot(query, pfull[h].astype(bf16), preferred_element_type=f32)
            carried_den = scale * jnp.sum(query.astype(f32) * rnback[h], axis=1, keepdims=True)
            prev = found[0][:, h * span : h * span + 1]
            peak = jnp.maximum(prev, reach)
            inner_factor = jnp.exp(reach - peak)
            outer_factor = jnp.exp(prev - peak)
            denom = inner_factor * inner_den + outer_factor * carried_den
            bound = jnp.maximum(jnp.abs(denom), jnp.exp(-(cumul_col + peak)))
            numer = inner_factor * inner[h] + outer_factor * carried
            o_ref[:, h * vd : (h + 1) * vd] = (numer / bound).astype(bf16)

    @pl.loop(1, ns)
    def _(d):
        o = seq_peer(d)
        small_copy(o, me).wait_send()
        for c in range(CHUNKS):
            state_copy(c, o, me).wait_send()
            back_copy(c, o, me).wait_send()

    for h in range(heads):
        @pl.when(me != h * per_head)
        def _(h=h):
            block_vector_copy(h, h * per_head, me).wait_send()

    @pl.when(owns_vector)
    def _():
        @pl.loop(1, ns)
        def _(d):
            vector_copy(seq_peer(d), myh).wait_send()

        @pl.loop(myg + 1 if UP else 1, ng)
        def _(d):
            group_vector_copy(d if UP else grp_peer(d), myg).wait_send()

    @pl.loop(myg + 1 if UP else 1, ng)
    def _(d):
        o = d if UP else grp_peer(d)
        group_small_copy(o, myg).wait_send()
        for c in range(CHUNKS):
            group_copy(c, o, myg).wait_send()


def on_device(ng, ns, queries, key_vectors, value_vectors, input_gate, forget_gate):
    heads, length = input_gate.shape
    kd = queries.shape[1] // heads
    vd = value_vectors.shape[1] // heads
    rp = kd * (vd // 128) // ns
    dma = pltpu.SemaphoreType.DMA

    def wide(*shape):
        return pltpu.VMEM(shape, jnp.float32)

    return pl.pallas_call(
        functools.partial(kernel, ng, ns, heads, kd, vd, length),
        out_shape=jax.ShapeDtypeStruct(value_vectors.shape, jnp.bfloat16),
        in_specs=[pl.BlockSpec(memory_space=pl.ANY)] * 5,
        out_specs=pl.BlockSpec(memory_space=pltpu.VMEM),
        scratch_shapes=[
            wide(heads, length), wide(heads, length),
            pltpu.VMEM(queries.shape, jnp.bfloat16),
            pltpu.VMEM(key_vectors.shape, jnp.bfloat16),
            pltpu.VMEM(value_vectors.shape, jnp.bfloat16),
            wide(heads, kd, vd), wide(heads, length, vd),
            wide(ns, heads, rp, 128), wide(ns, heads, rp, 128), wide(heads, kd, vd),
            wide(heads, rp, 128), wide(ng, heads, rp, 128),
            wide(1, 128), wide(ns, 1, 128), wide(1, 128), wide(ng, 1, 128),
            wide(heads, 1, 128), wide(ns, 1, 128), wide(1, 128), wide(ng, 1, 128),
            wide(ns, 1, 128), wide(heads, 1, 128), wide(ns, 128),
            wide(ns, 128), wide(ns, 128), wide(ns, 128), wide(ns, 128),
            wide(heads, ns, 128), wide(heads, ns, 128), wide(heads, ns, 128), wide(heads, ns, 128),
            wide(ng, 128), wide(ng, 128), wide(heads, ng, 128), wide(heads, ng, 128),
            dma((5,)),
            dma((CHUNKS, ns)), dma((CHUNKS, ns)),
            dma((ns,)), dma((ns,)),
            dma((CHUNKS, ng)), dma((CHUNKS, ng)),
            dma((ng,)), dma((ng,)),
            dma((CHUNKS, ns)), dma((CHUNKS, ns)),
            dma((ns,)), dma((heads,)),
            dma((heads,)), dma((ns,)), dma((ng,)), dma((ng,)),
        ],
        compiler_params=pltpu.CompilerParams(collective_id=0, has_side_effects=True),
        name="mlstm_layer",
    )(queries, key_vectors, value_vectors, input_gate, forget_gate)


def solution(mesh):
    return jax.shard_map(
        functools.partial(on_device, mesh.shape["grp"], mesh.shape["seq"]),
        mesh=mesh,
        in_specs=(
            P(("grp", "seq"), None),
            P(("grp", "seq"), None),
            P(("grp", "seq"), None),
            P(None, ("grp", "seq")),
            P(None, ("grp", "seq")),
        ),
        out_specs=P(("grp", "seq"), None),
        check_vma=False,
    )
```

```python
import functools

import jax
import jax.numpy as jnp
from jax import lax
from jax.experimental import pallas as pl
from jax.experimental.pallas import tpu as pltpu
from jax.sharding import PartitionSpec as P

MESH = pl.DeviceIdType.MESH
FLOOR = -1e30
SIZES = (2, 2)
UNROLL = 1


def split3(x):
    hi = x.astype(jnp.bfloat16)
    rest = x - hi.astype(jnp.float32)
    mid = rest.astype(jnp.bfloat16)
    low = (rest - mid.astype(jnp.float32)).astype(jnp.bfloat16)
    return hi, mid, low


def kernel(
    ng, ns, heads, kd, vd, length,
    q_hbm, k_hbm, v_hbm, ig_hbm, fg_hbm, o_ref,
    ig, fg, qv, kv, vv, state, inner, rbuf, pbuf, pfull, gsend, grecv,
    small, rsmall, gsmall, grsmall, vec, rvec, gvec, grvec, nback, rnback, nrows,
    rows_a, rows_b, rows_t, rows_d, wide_a, wide_b, wide_c, wide_d, group_a, group_b, group_wide_a, group_wide_b,
    in_sem, s1, r1, ss, rs, sg, rg, sgs, rgs, s3, r3, sn, rn, sv, rv, sgv, rgv,
):
    f32, bf16 = jnp.float32, jnp.bfloat16
    chunks = len(SIZES)
    first = [sum(SIZES[:c]) for c in range(chunks + 1)]
    rp = kd * (vd // 128) // ns
    cols = vd // 128
    per_head = ns // heads
    span = 64 // heads
    scale = kd ** (-0.5)
    myg = lax.axis_index("grp")
    me = lax.axis_index("seq")
    myh = me // per_head
    owns_vector = (me & (per_head - 1)) == 0

    def seq_peer(d):
        return (me + d) & (ns - 1)

    def grp_peer(d):
        return (myg + d) & (ng - 1)

    def each_peer(do):
        if UNROLL:
            for d in range(1, ns):
                do(seq_peer(d))
        else:

            @pl.loop(1, ns)
            def _(d):
                do(seq_peer(d))

    copies = [
        pltpu.make_async_copy(src, dst, in_sem.at[n])
        for n, (src, dst) in enumerate(
            ((fg_hbm, fg), (ig_hbm, ig), (k_hbm, kv), (v_hbm, vv), (q_hbm, qv))
        )
    ]
    for copy in copies:
        copy.start()

    barrier = pltpu.get_barrier_semaphore()

    def greet(device):
        pl.semaphore_signal(barrier, inc=1, device_id=device, device_id_type=MESH)

    each_peer(lambda o: greet((myg, o)))
    for d in range(1, ng):
        greet((grp_peer(d), me))

    zero = jnp.zeros((1, 128), f32)

    @pl.loop(myg + 1, ng)
    def _(g):
        grsmall[g] = zero
        grvec[g] = zero
        for h in range(heads):
            grecv[g, h] = jnp.zeros((rp, 128), f32)

    lane = lax.broadcasted_iota(jnp.int32, (heads, 128), 1)
    head_row = lax.broadcasted_iota(jnp.int32, (heads, 128), 0)
    rows = lax.broadcasted_iota(jnp.int32, (length, length), 0)
    lanes = lax.broadcasted_iota(jnp.int32, (length, length), 1)

    def slice_of(ref, c, o):
        row = pl.multiple_of((o >> (cols.bit_length() - 1)) * rp, 8)
        col = pl.multiple_of((o & (cols - 1)) * 128, 128)
        return ref.at[pl.ds(first[c], SIZES[c]), pl.ds(row, rp), pl.ds(col, 128)]

    def part(c):
        return pl.ds(first[c], SIZES[c])

    def remote(src, dst, send, recv, device):
        return pltpu.make_async_remote_copy(
            src_ref=src, dst_ref=dst, send_sem=send, recv_sem=recv, device_id=device, device_id_type=MESH
        )

    def small_copy(o, slot):
        return remote(
            small, rsmall.at[slot], ss.at[0], rs.at[0], (myg, o)
        )

    def block_vector_copy(h, o, slot):
        return remote(vec.at[h], rvec.at[slot], sv.at[h], rv.at[0], (myg, o))

    def group_vector_copy(o, slot):
        return remote(gvec, grvec.at[slot], sgv.at[o], rgv.at[slot], (o, me))

    def state_copy(c, o, slot):
        return remote(
            slice_of(state, c, o), rbuf.at[slot, part(c)], s1.at[c], r1.at[c], (myg, o)
        )

    def back_copy(c, o, slot):
        return remote(
            pbuf.at[o, part(c)], slice_of(pfull, c, slot), s3.at[c], r3.at[c], (myg, o)
        )

    def vector_copy(o, h):
        return remote(nback.at[o], rnback.at[h], sn.at[0], rn.at[h], (myg, o))

    others = pl.ds(0, ns - 1)

    def all_small():
        return remote(rsmall.at[others], rsmall.at[others], ss.at[0], rs.at[0], (myg, me))

    def all_state(c):
        ref = rbuf.at[others, part(c)]
        return remote(ref, ref, s1.at[c], r1.at[c], (myg, me))

    def all_back(c):
        ref = pbuf.at[others, part(c)]
        return remote(ref, ref, s3.at[c], r3.at[c], (myg, me))

    def all_block_vectors():
        return remote(rvec.at[others], rvec.at[others], sv.at[0], rv.at[0], (myg, me))

    def all_vectors():
        return remote(nback.at[others], nback.at[others], sn.at[0], rn.at[0], (myg, me))

    def group_small_copy(o, slot):
        return remote(gsmall, grsmall.at[slot], sgs.at[o], rgs.at[slot], (o, me))

    def group_copy(c, o, slot):
        return remote(
            gsend.at[part(c)], grecv.at[slot, part(c)], sg.at[c, o], rg.at[c, slot], (o, me)
        )

    upper = jnp.where(rows <= lanes, 1.0, 0.0).astype(bf16)
    copies[0].wait()
    copies[1].wait()
    forget = fg[...]
    logf = jnp.minimum(forget, 0.0) - jnp.log1p(jnp.exp(-jnp.abs(forget)))

    def exact_rows(values, matrix):
        hi, mid, low = split3(values)
        lhs = jnp.concatenate([hi, mid, low, jnp.zeros_like(low)], axis=0)
        out = jnp.dot(lhs, matrix, preferred_element_type=f32)
        n = values.shape[0]
        return out[0:n] + out[n : 2 * n] + out[2 * n : 3 * n]

    cumul = exact_rows(logf, upper)
    level = ig[...] - cumul
    decay = cumul[:, length - 1 : length]
    level_top = jnp.max(level, axis=1, keepdims=True)
    weight = jnp.exp(level - level_top)
    top = decay + level_top

    mine = jnp.where(lane < 64, decay, top)
    pick = lax.div(lax.rem(lane, 64), span) == head_row
    scalars = jnp.sum(jnp.where(pick, mine, 0.0), axis=0, keepdims=True)

    copies[2].wait()
    copies[3].wait()

    def local_state(c):
        for h in range(first[c], first[c + 1]):
            turned = kv[:, h * kd : (h + 1) * kd].astype(f32).T
            scaled = (turned * weight[h : h + 1, :]).astype(bf16)
            state[h] = jnp.dot(scaled, vv[:, h * vd : (h + 1) * vd], preferred_element_type=f32)
        rbuf[me, first[c] : first[c + 1]] = slice_of(state, c, me)[...]

    def send_state(c):
        each_peer(lambda o: state_copy(c, o, me).start())

    small[...] = scalars
    rsmall[me] = scalars
    local_state(0)
    pl.semaphore_wait(barrier, ns - 1 + ng - 1)

    each_peer(lambda o: small_copy(o, me).start())

    send_state(0)
    for c in range(1, chunks):
        local_state(c)
        send_state(c)

    for h in range(heads):
        vector = exact_rows(weight, kv[:, h * kd : (h + 1) * kd])
        vec[h] = vector[h : h + 1, :]
    for h in range(heads):
        @pl.when(me == h * per_head)
        def _(h=h):
            rvec[me] = vec[h]

        @pl.when(me != h * per_head)
        def _(h=h):
            block_vector_copy(h, h * per_head, me).start()

    copies[4].wait()
    columns = []
    for h in range(heads):
        scores = scale * lax.dot_general(
            qv[:, h * kd : (h + 1) * kd], kv[:, h * kd : (h + 1) * kd],
            (((1,), (1,)), ((), ())), preferred_element_type=f32,
        )
        masked = jnp.where(rows >= lanes, level[h : h + 1, :], -jnp.inf)
        reach = jnp.max(masked, axis=1, keepdims=True)
        weighted = jnp.exp(masked - reach) * scores
        inner_den = jnp.sum(weighted, axis=1, keepdims=True)
        cumul_col = jnp.sum(
            jnp.where(rows == lanes, cumul[h : h + 1, :], 0.0), axis=1, keepdims=True
        )
        inner[h] = jnp.dot(
            weighted.astype(bf16), vv[:, h * vd : (h + 1) * vd], preferred_element_type=f32
        )
        columns.append((reach, inner_den, cumul_col))

    all_small().wait_recv()

    def widen(out, source):
        for h in range(heads):
            out[h] = jnp.broadcast_to(source[:, h * span : h * span + 1], (ns, 128))

    run_top = jnp.full((1, 128), FLOOR, f32)
    run_dec = jnp.zeros((1, 128), f32)
    for i in range(ns):
        row = rsmall[i]
        top_i = pltpu.roll(row, 64, 1)
        rows_t[i : i + 1, :] = run_top
        rows_d[i : i + 1, :] = run_dec
        early = run_top + row
        joined = jnp.maximum(early, top_i)
        rows_a[i : i + 1, :] = early - joined
        rows_b[i : i + 1, :] = top_i - joined
        run_top = joined
        run_dec = run_dec + row
    lane1 = lax.broadcasted_iota(jnp.int32, (1, 128), 1)
    widen(wide_a, jnp.exp(rows_a[...]))
    widen(wide_b, jnp.exp(rows_b[...]))

    total = jnp.where(lane1 < 64, run_dec, pltpu.roll(run_top, 64, 1))
    gsmall[...] = total
    grsmall[myg] = total

    @pl.loop(myg + 1, ng)
    def _(d):
        group_small_copy(d, myg).start()

    def scan_vector():
        @pl.when(owns_vector)
        def _():
            all_block_vectors().wait_recv()

            run_vec = jnp.zeros((1, 128), f32)
            for i in range(ns):
                nrows[i : i + 1, :] = run_vec
                run_vec = wide_a[myh, i : i + 1, :] * run_vec + wide_b[myh, i : i + 1, :] * rvec[i]
            gvec[...] = run_vec
            grvec[myg] = run_vec

            @pl.loop(myg + 1, ng)
            def _(d):
                group_vector_copy(d, myg).start()

    def scan(c):
        all_state(c).wait_recv()

        for h in range(first[c], first[c + 1]):
            run = jnp.zeros((rp, 128), f32)
            for i in range(ns):
                pbuf[i, h] = run
                run = wide_a[h, i : i + 1, :] * run + wide_b[h, i : i + 1, :] * rbuf[i, h]
            gsend[h] = run
        grecv[myg, first[c] : first[c + 1]] = gsend[first[c] : first[c + 1]]

        @pl.loop(myg + 1, ng)
        def _(d):
            group_copy(c, d, myg).start()

    order = [(what, c) for c in range(chunks) for what in ("scan", "back")]
    order = order[:1] + [("group", 0)] + order[1:-1] + [("vector", 0)] + order[-1:] + [("return", 0)]

    found = []

    def before_group():
        @pl.loop(0, myg)
        def _(d):
            o = d
            group_small_copy(o, o).wait_recv()

        before_top = jnp.full((1, 128), FLOOR, f32)
        for g in range(ng):
            row = grsmall[g]
            top_g = pltpu.roll(row, 64, 1)
            counts = g < myg
            early = before_top + row
            joined = jnp.maximum(early, top_g)
            a = jnp.where(counts, jnp.exp(early - joined), 1.0)
            b = jnp.where(counts, jnp.exp(top_g - joined), 0.0)
            before_top = jnp.where(counts, joined, before_top)
            group_a[g : g + 1, :] = a
            group_b[g : g + 1, :] = b
        tops = rows_t[...]
        early = before_top + rows_d[...]
        full = jnp.maximum(early, tops)
        rows_t[...] = full
        found.append(rows_t[pl.ds(me, 1), :])
        widen(wide_c, jnp.exp(early - full))
        widen(wide_d, jnp.exp(tops - full))
        for h in range(heads):
            group_wide_a[h] = jnp.broadcast_to(group_a[:, h * span : h * span + 1], (ng, 128))
            group_wide_b[h] = jnp.broadcast_to(group_b[:, h * span : h * span + 1], (ng, 128))

    def return_vector():
        @pl.when(owns_vector)
        def _():
            @pl.loop(0, myg)
            def _(d):
                o = d
                group_vector_copy(o, o).wait_recv()

            before = jnp.zeros((1, 128), f32)
            for g in range(ng):
                before = (
                    group_wide_a[myh, g : g + 1, :] * before
                    + group_wide_b[myh, g : g + 1, :] * grvec[g]
                )
            vectors = wide_c[myh] * before + wide_d[myh] * nrows[...]
            for i in range(ns):
                nback[i] = vectors[i : i + 1, :]
            rnback[myh] = nback[me]

            @pl.loop(1, ns)
            def _(d):
                vector_copy(seq_peer(d), myh).start()

    def back(c):
        @pl.loop(0, myg)
        def _(d):
            o = d
            group_copy(c, o, o).wait_recv()

        for h in range(first[c], first[c + 1]):
            run = jnp.zeros((rp, 128), f32)
            for g in range(ng):
                run = group_wide_a[h, g : g + 1, :] * run + group_wide_b[h, g : g + 1, :] * grecv[g, h]
            for i in range(ns):
                pbuf[i, h] = wide_c[h, i : i + 1, :] * run + wide_d[h, i : i + 1, :] * pbuf[i, h]

        each_peer(lambda o: back_copy(c, o, me).start())
        slice_of(pfull, c, me)[...] = pbuf[me, first[c] : first[c + 1]]

    for what, c in order:
        if what == "scan":
            scan(c)
        elif what == "back":
            back(c)
        elif what == "group":
            before_group()
        elif what == "vector":
            scan_vector()
        else:
            return_vector()

    for h in range(heads):
        @pl.when(me != h * per_head)
        def _(h=h):
            vector_copy(h * per_head, h).wait_recv()

    for c in range(chunks):
        all_back(c).wait_recv()

        for h in range(first[c], first[c + 1]):
            reach, inner_den, cumul_col = columns[h]
            query = qv[:, h * kd : (h + 1) * kd]
            carried = scale * jnp.dot(query, pfull[h].astype(bf16), preferred_element_type=f32)
            carried_den = scale * jnp.sum(query.astype(f32) * rnback[h], axis=1, keepdims=True)
            prev = found[0][:, h * span : h * span + 1]
            peak = jnp.maximum(prev, reach)
            inner_factor = jnp.exp(reach - peak)
            outer_factor = jnp.exp(prev - peak)
            denom = inner_factor * inner_den + outer_factor * carried_den
            bound = jnp.maximum(jnp.abs(denom), jnp.exp(-(cumul_col + peak)))
            numer = inner_factor * inner[h] + outer_factor * carried
            o_ref[:, h * vd : (h + 1) * vd] = (numer / bound).astype(bf16)

    all_small().wait_send()
    for c in range(chunks):
        all_state(c).wait_send()
        all_back(c).wait_send()

    for h in range(heads):
        @pl.when(me != h * per_head)
        def _(h=h):
            block_vector_copy(h, h * per_head, me).wait_send()

    @pl.when(owns_vector)
    def _():
        all_vectors().wait_send()

        @pl.loop(myg + 1, ng)
        def _(d):
            group_vector_copy(d, myg).wait_send()

    @pl.loop(myg + 1, ng)
    def _(d):
        o = d
        group_small_copy(o, myg).wait_send()
        for c in range(chunks):
            group_copy(c, o, myg).wait_send()


def on_device(ng, ns, queries, key_vectors, value_vectors, input_gate, forget_gate):
    heads, length = input_gate.shape
    kd = queries.shape[1] // heads
    vd = value_vectors.shape[1] // heads
    rp = kd * (vd // 128) // ns
    dma = pltpu.SemaphoreType.DMA

    def wide(*shape):
        return pltpu.VMEM(shape, jnp.float32)

    return pl.pallas_call(
        functools.partial(kernel, ng, ns, heads, kd, vd, length),
        out_shape=pltpu.VMEM(value_vectors.shape, jnp.bfloat16),
        in_specs=[pl.BlockSpec(memory_space=pl.ANY)] * 5,
        out_specs=pl.BlockSpec(memory_space=pltpu.VMEM),
        scratch_shapes=[
            wide(heads, length), wide(heads, length),
            pltpu.VMEM(queries.shape, jnp.bfloat16),
            pltpu.VMEM(key_vectors.shape, jnp.bfloat16),
            pltpu.VMEM(value_vectors.shape, jnp.bfloat16),
            wide(heads, kd, vd), wide(heads, length, vd),
            wide(ns, heads, rp, 128), wide(ns, heads, rp, 128), wide(heads, kd, vd),
            wide(heads, rp, 128), wide(ng, heads, rp, 128),
            wide(1, 128), wide(ns, 1, 128), wide(1, 128), wide(ng, 1, 128),
            wide(heads, 1, 128), wide(ns, 1, 128), wide(1, 128), wide(ng, 1, 128),
            wide(ns, 1, 128), wide(heads, 1, 128), wide(ns, 128),
            wide(ns, 128), wide(ns, 128), wide(ns, 128), wide(ns, 128),
            wide(heads, ns, 128), wide(heads, ns, 128), wide(heads, ns, 128), wide(heads, ns, 128),
            wide(ng, 128), wide(ng, 128), wide(heads, ng, 128), wide(heads, ng, 128),
            dma((5,)),
            dma((len(SIZES),)), dma((len(SIZES),)), dma((1,)), dma((1,)),
            dma((len(SIZES), ng)), dma((len(SIZES), ng)), dma((ng,)), dma((ng,)),
            dma((len(SIZES),)), dma((len(SIZES),)), dma((1,)), dma((heads,)),
            dma((heads,)), dma((1,)), dma((ng,)), dma((ng,)),
        ],
        compiler_params=pltpu.CompilerParams(collective_id=0, has_side_effects=True),
        name="mlstm_layer",
    )(queries, key_vectors, value_vectors, input_gate, forget_gate)


def solution(mesh):
    return jax.shard_map(
        functools.partial(on_device, mesh.shape["grp"], mesh.shape["seq"]),
        mesh=mesh,
        in_specs=(
            P(("grp", "seq"), None),
            P(("grp", "seq"), None),
            P(("grp", "seq"), None),
            P(None, ("grp", "seq")),
            P(None, ("grp", "seq")),
        ),
        out_specs=P(("grp", "seq"), None),
        check_vma=False,
    )
```

```python
import functools

import jax
import jax.numpy as jnp
from jax import lax
from jax.experimental import pallas as pl
from jax.experimental.pallas import tpu as pltpu
from jax.sharding import PartitionSpec as P

MESH = pl.DeviceIdType.MESH
FLOOR = -1e30
SIZES = (2, 2)
COLUMNS = (0, 1, 2, 3, 4, 7, 5, 6)


def split3(x):
    hi = x.astype(jnp.bfloat16)
    rest = x - hi.astype(jnp.float32)
    mid = rest.astype(jnp.bfloat16)
    low = (rest - mid.astype(jnp.float32)).astype(jnp.bfloat16)
    return hi, mid, low


def kernel(
    ng, ns, heads, kd, vd, length,
    q_hbm, k_hbm, v_hbm, ig_hbm, fg_hbm, o_ref,
    ig, fg, qv, kv, vv, state, inner, rbuf, pbuf, pfull, gsend, grecv,
    small, rsmall, gsmall, grsmall, vec, rvec, gvec, grvec, nback, rnback, nrows,
    rows_a, rows_b, rows_t, rows_d, wide_a, wide_b, wide_c, wide_d, group_a, group_b, group_wide_a, group_wide_b,
    in_sem, s1, r1, ss, rs, sg, rg, sgs, rgs, s3, r3, sn, rn, sv, rv, sgv, rgv,
):
    f32, bf16 = jnp.float32, jnp.bfloat16
    chunks = len(SIZES)
    first = [sum(SIZES[:c]) for c in range(chunks + 1)]
    rp = kd * (vd // 128) // ns
    cols = vd // 128
    per_head = ns // heads
    span = 64 // heads
    scale = kd ** (-0.5)
    myg = lax.axis_index("grp")
    me = lax.axis_index("seq")
    myh = me // per_head
    owns_vector = (me & (per_head - 1)) == 0

    def seq_peer(d):
        return (me + d) & (ns - 1)

    def grp_peer(d):
        return (myg + d) & (ng - 1)

    zdim = min(8, ns)
    ydim = ns // zdim
    zbits = zdim.bit_length() - 1
    y, z = me >> zbits, me & (zdim - 1)

    def each_peer(do):
        for d in range(1, ns):
            do(seq_peer(d))

    def far_first(do):
        def far(n, size):
            return min(n, size - n)

        steps = [(dy, dz) for dy in range(ydim) for dz in range(zdim) if dy or dz]
        steps.sort(key=lambda t: (far(t[1], zdim), far(t[0], ydim)), reverse=True)
        for dy, dz in steps:
            do((((y + dy) & (ydim - 1)) << zbits) | ((z + dz) & (zdim - 1)))

    def to_columns(do, columns):
        for to in columns:
            for dy in range(ydim):
                o = (((y + dy) & (ydim - 1)) << zbits) | to
                if dy:
                    do(o)
                else:
                    pl.when(to != z)(functools.partial(do, o))

    copies = [
        pltpu.make_async_copy(src, dst, in_sem.at[n])
        for n, (src, dst) in enumerate(
            ((fg_hbm, fg), (ig_hbm, ig), (k_hbm, kv), (v_hbm, vv), (q_hbm, qv))
        )
    ]
    for copy in copies:
        copy.start()

    barrier = pltpu.get_barrier_semaphore()

    def greet(device):
        pl.semaphore_signal(barrier, inc=1, device_id=device, device_id_type=MESH)

    each_peer(lambda o: greet((myg, o)))
    for d in range(1, ng):
        greet((grp_peer(d), me))

    zero = jnp.zeros((1, 128), f32)

    @pl.loop(myg + 1, ng)
    def _(g):
        grsmall[g] = zero
        grvec[g] = zero
        for h in range(heads):
            grecv[g, h] = jnp.zeros((rp, 128), f32)

    lane = lax.broadcasted_iota(jnp.int32, (heads, 128), 1)
    head_row = lax.broadcasted_iota(jnp.int32, (heads, 128), 0)
    rows = lax.broadcasted_iota(jnp.int32, (length, length), 0)
    lanes = lax.broadcasted_iota(jnp.int32, (length, length), 1)

    def slice_of(ref, c, o):
        row = pl.multiple_of((o >> (cols.bit_length() - 1)) * rp, 8)
        col = pl.multiple_of((o & (cols - 1)) * 128, 128)
        return ref.at[pl.ds(first[c], SIZES[c]), pl.ds(row, rp), pl.ds(col, 128)]

    def part(c):
        return pl.ds(first[c], SIZES[c])

    def remote(src, dst, send, recv, device):
        return pltpu.make_async_remote_copy(
            src_ref=src, dst_ref=dst, send_sem=send, recv_sem=recv, device_id=device, device_id_type=MESH
        )

    def small_copy(o, slot):
        return remote(
            small, rsmall.at[slot], ss.at[0], rs.at[0], (myg, o)
        )

    def block_vector_copy(h, o, slot):
        return remote(vec.at[h], rvec.at[slot], sv.at[h], rv.at[0], (myg, o))

    def group_vector_copy(o, slot):
        return remote(gvec, grvec.at[slot], sgv.at[o], rgv.at[slot], (o, me))

    def state_copy(c, o, slot):
        return remote(
            slice_of(state, c, o), rbuf.at[slot, part(c)], s1.at[c], r1.at[c], (myg, o)
        )

    def back_copy(c, o, slot):
        return remote(
            pbuf.at[o, part(c)], slice_of(pfull, c, slot), s3.at[c], r3.at[c], (myg, o)
        )

    def vector_copy(o, h):
        return remote(nback.at[o], rnback.at[h], sn.at[0], rn.at[h], (myg, o))

    others = pl.ds(0, ns - 1)

    def all_small():
        return remote(rsmall.at[others], rsmall.at[others], ss.at[0], rs.at[0], (myg, me))

    def all_state(c):
        ref = rbuf.at[others, part(c)]
        return remote(ref, ref, s1.at[c], r1.at[c], (myg, me))

    def all_back(c):
        ref = pbuf.at[others, part(c)]
        return remote(ref, ref, s3.at[c], r3.at[c], (myg, me))

    def all_block_vectors():
        return remote(rvec.at[others], rvec.at[others], sv.at[0], rv.at[0], (myg, me))

    def all_vectors():
        return remote(nback.at[others], nback.at[others], sn.at[0], rn.at[0], (myg, me))

    def group_small_copy(o, slot):
        return remote(gsmall, grsmall.at[slot], sgs.at[o], rgs.at[slot], (o, me))

    def group_copy(c, o, slot):
        return remote(
            gsend.at[part(c)], grecv.at[slot, part(c)], sg.at[c, o], rg.at[c, slot], (o, me)
        )

    upper = jnp.where(rows <= lanes, 1.0, 0.0).astype(bf16)
    copies[0].wait()
    copies[1].wait()
    forget = fg[...]
    logf = jnp.minimum(forget, 0.0) - jnp.log1p(jnp.exp(-jnp.abs(forget)))

    def exact_rows(values, matrix):
        hi, mid, low = split3(values)
        lhs = jnp.concatenate([hi, mid, low, jnp.zeros_like(low)], axis=0)
        out = jnp.dot(lhs, matrix, preferred_element_type=f32)
        n = values.shape[0]
        return out[0:n] + out[n : 2 * n] + out[2 * n : 3 * n]

    cumul = exact_rows(logf, upper)
    level = ig[...] - cumul
    decay = cumul[:, length - 1 : length]
    level_top = jnp.max(level, axis=1, keepdims=True)
    weight = jnp.exp(level - level_top)
    top = decay + level_top

    mine = jnp.where(lane < 64, decay, top)
    pick = lax.div(lax.rem(lane, 64), span) == head_row
    scalars = jnp.sum(jnp.where(pick, mine, 0.0), axis=0, keepdims=True)

    copies[2].wait()
    copies[3].wait()

    def local_state(c):
        for h in range(first[c], first[c + 1]):
            turned = kv[:, h * kd : (h + 1) * kd].astype(f32).T
            scaled = (turned * weight[h : h + 1, :]).astype(bf16)
            state[h] = jnp.dot(scaled, vv[:, h * vd : (h + 1) * vd], preferred_element_type=f32)
        rbuf[me, first[c] : first[c + 1]] = slice_of(state, c, me)[...]

    def send_state(c):
        far_first(lambda o: state_copy(c, o, me).start())

    small[...] = scalars
    rsmall[me] = scalars
    local_state(0)
    pl.semaphore_wait(barrier, ns - 1 + ng - 1)

    each_peer(lambda o: small_copy(o, me).start())

    send_state(0)
    for c in range(1, chunks):
        local_state(c)
        send_state(c)

    for h in range(heads):
        vector = exact_rows(weight, kv[:, h * kd : (h + 1) * kd])
        vec[h] = vector[h : h + 1, :]
    for h in range(heads):
        @pl.when(me == h * per_head)
        def _(h=h):
            rvec[me] = vec[h]

        @pl.when(me != h * per_head)
        def _(h=h):
            block_vector_copy(h, h * per_head, me).start()

    copies[4].wait()
    columns = []
    for h in range(heads):
        scores = scale * lax.dot_general(
            qv[:, h * kd : (h + 1) * kd], kv[:, h * kd : (h + 1) * kd],
            (((1,), (1,)), ((), ())), preferred_element_type=f32,
        )
        masked = jnp.where(rows >= lanes, level[h : h + 1, :], -jnp.inf)
        reach = jnp.max(masked, axis=1, keepdims=True)
        weighted = jnp.exp(masked - reach) * scores
        inner_den = jnp.sum(weighted, axis=1, keepdims=True)
        cumul_col = jnp.sum(
            jnp.where(rows == lanes, cumul[h : h + 1, :], 0.0), axis=1, keepdims=True
        )
        inner[h] = jnp.dot(
            weighted.astype(bf16), vv[:, h * vd : (h + 1) * vd], preferred_element_type=f32
        )
        columns.append((reach, inner_den, cumul_col))

    all_small().wait_recv()

    def widen(out, source):
        for h in range(heads):
            out[h] = jnp.broadcast_to(source[:, h * span : h * span + 1], (ns, 128))

    run_top = jnp.full((1, 128), FLOOR, f32)
    run_dec = jnp.zeros((1, 128), f32)
    for i in range(ns):
        row = rsmall[i]
        top_i = pltpu.roll(row, 64, 1)
        rows_t[i : i + 1, :] = run_top
        rows_d[i : i + 1, :] = run_dec
        early = run_top + row
        joined = jnp.maximum(early, top_i)
        rows_a[i : i + 1, :] = early - joined
        rows_b[i : i + 1, :] = top_i - joined
        run_top = joined
        run_dec = run_dec + row
    lane1 = lax.broadcasted_iota(jnp.int32, (1, 128), 1)
    widen(wide_a, jnp.exp(rows_a[...]))
    widen(wide_b, jnp.exp(rows_b[...]))

    total = jnp.where(lane1 < 64, run_dec, pltpu.roll(run_top, 64, 1))
    gsmall[...] = total
    grsmall[myg] = total

    @pl.loop(myg + 1, ng)
    def _(d):
        group_small_copy(d, myg).start()

    def scan_vector():
        @pl.when(owns_vector)
        def _():
            all_block_vectors().wait_recv()

            run_vec = jnp.zeros((1, 128), f32)
            for i in range(ns):
                nrows[i : i + 1, :] = run_vec
                run_vec = wide_a[myh, i : i + 1, :] * run_vec + wide_b[myh, i : i + 1, :] * rvec[i]
            gvec[...] = run_vec
            grvec[myg] = run_vec

            @pl.loop(myg + 1, ng)
            def _(d):
                group_vector_copy(d, myg).start()

    def scan(c):
        all_state(c).wait_recv()

        for h in range(first[c], first[c + 1]):
            run = jnp.zeros((rp, 128), f32)
            for i in range(ns):
                pbuf[i, h] = run
                run = wide_a[h, i : i + 1, :] * run + wide_b[h, i : i + 1, :] * rbuf[i, h]
            gsend[h] = run
        grecv[myg, first[c] : first[c + 1]] = gsend[first[c] : first[c + 1]]

        @pl.loop(myg + 1, ng)
        def _(d):
            group_copy(c, d, myg).start()

    order = [(what, c) for c in range(chunks) for what in ("scan", "back")]
    order = order[:1] + [("group", 0)] + order[1:-1] + [("vector", 0)] + order[-1:] + [("return", 0)]

    found = []

    def before_group():
        @pl.loop(0, myg)
        def _(d):
            o = d
            group_small_copy(o, o).wait_recv()

        before_top = jnp.full((1, 128), FLOOR, f32)
        for g in range(ng):
            row = grsmall[g]
            top_g = pltpu.roll(row, 64, 1)
            counts = g < myg
            early = before_top + row
            joined = jnp.maximum(early, top_g)
            a = jnp.where(counts, jnp.exp(early - joined), 1.0)
            b = jnp.where(counts, jnp.exp(top_g - joined), 0.0)
            before_top = jnp.where(counts, joined, before_top)
            group_a[g : g + 1, :] = a
            group_b[g : g + 1, :] = b
        tops = rows_t[...]
        early = before_top + rows_d[...]
        full = jnp.maximum(early, tops)
        rows_t[...] = full
        found.append(rows_t[pl.ds(me, 1), :])
        widen(wide_c, jnp.exp(early - full))
        widen(wide_d, jnp.exp(tops - full))
        for h in range(heads):
            group_wide_a[h] = jnp.broadcast_to(group_a[:, h * span : h * span + 1], (ng, 128))
            group_wide_b[h] = jnp.broadcast_to(group_b[:, h * span : h * span + 1], (ng, 128))

    def return_vector():
        @pl.when(owns_vector)
        def _():
            @pl.loop(0, myg)
            def _(d):
                o = d
                group_vector_copy(o, o).wait_recv()

            before = jnp.zeros((1, 128), f32)
            for g in range(ng):
                before = (
                    group_wide_a[myh, g : g + 1, :] * before
                    + group_wide_b[myh, g : g + 1, :] * grvec[g]
                )
            vectors = wide_c[myh] * before + wide_d[myh] * nrows[...]
            for i in range(ns):
                nback[i] = vectors[i : i + 1, :]
            rnback[myh] = nback[me]

            @pl.loop(1, ns)
            def _(d):
                vector_copy(seq_peer(d), myh).start()

    def back(c):
        @pl.loop(0, myg)
        def _(d):
            o = d
            group_copy(c, o, o).wait_recv()

        for h in range(first[c], first[c + 1]):
            run = jnp.zeros((rp, 128), f32)
            for g in range(ng):
                run = group_wide_a[h, g : g + 1, :] * run + group_wide_b[h, g : g + 1, :] * grecv[g, h]
            for i in range(ns):
                pbuf[i, h] = wide_c[h, i : i + 1, :] * run + wide_d[h, i : i + 1, :] * pbuf[i, h]

        to_columns(lambda o: back_copy(c, o, me).start(), COLUMNS)
        slice_of(pfull, c, me)[...] = pbuf[me, first[c] : first[c + 1]]

    for what, c in order:
        if what == "scan":
            scan(c)
        elif what == "back":
            back(c)
        elif what == "group":
            before_group()
        elif what == "vector":
            scan_vector()
        else:
            return_vector()

    for h in range(heads):
        @pl.when(me != h * per_head)
        def _(h=h):
            vector_copy(h * per_head, h).wait_recv()

    for c in range(chunks):
        all_back(c).wait_recv()

        for h in range(first[c], first[c + 1]):
            reach, inner_den, cumul_col = columns[h]
            query = qv[:, h * kd : (h + 1) * kd]
            carried = scale * jnp.dot(query, pfull[h].astype(bf16), preferred_element_type=f32)
            carried_den = scale * jnp.sum(query.astype(f32) * rnback[h], axis=1, keepdims=True)
            prev = found[0][:, h * span : h * span + 1]
            peak = jnp.maximum(prev, reach)
            inner_factor = jnp.exp(reach - peak)
            outer_factor = jnp.exp(prev - peak)
            denom = inner_factor * inner_den + outer_factor * carried_den
            bound = jnp.maximum(jnp.abs(denom), jnp.exp(-(cumul_col + peak)))
            numer = inner_factor * inner[h] + outer_factor * carried
            o_ref[:, h * vd : (h + 1) * vd] = (numer / bound).astype(bf16)

    all_small().wait_send()
    for c in range(chunks):
        all_state(c).wait_send()
        all_back(c).wait_send()

    for h in range(heads):
        @pl.when(me != h * per_head)
        def _(h=h):
            block_vector_copy(h, h * per_head, me).wait_send()

    @pl.when(owns_vector)
    def _():
        all_vectors().wait_send()

        @pl.loop(myg + 1, ng)
        def _(d):
            group_vector_copy(d, myg).wait_send()

    @pl.loop(myg + 1, ng)
    def _(d):
        o = d
        group_small_copy(o, myg).wait_send()
        for c in range(chunks):
            group_copy(c, o, myg).wait_send()


def on_device(ng, ns, queries, key_vectors, value_vectors, input_gate, forget_gate):
    heads, length = input_gate.shape
    kd = queries.shape[1] // heads
    vd = value_vectors.shape[1] // heads
    rp = kd * (vd // 128) // ns
    dma = pltpu.SemaphoreType.DMA

    def wide(*shape):
        return pltpu.VMEM(shape, jnp.float32)

    return pl.pallas_call(
        functools.partial(kernel, ng, ns, heads, kd, vd, length),
        out_shape=pltpu.VMEM(value_vectors.shape, jnp.bfloat16),
        in_specs=[pl.BlockSpec(memory_space=pl.ANY)] * 5,
        out_specs=pl.BlockSpec(memory_space=pltpu.VMEM),
        scratch_shapes=[
            wide(heads, length), wide(heads, length),
            pltpu.VMEM(queries.shape, jnp.bfloat16),
            pltpu.VMEM(key_vectors.shape, jnp.bfloat16),
            pltpu.VMEM(value_vectors.shape, jnp.bfloat16),
            wide(heads, kd, vd), wide(heads, length, vd),
            wide(ns, heads, rp, 128), wide(ns, heads, rp, 128), wide(heads, kd, vd),
            wide(heads, rp, 128), wide(ng, heads, rp, 128),
            wide(1, 128), wide(ns, 1, 128), wide(1, 128), wide(ng, 1, 128),
            wide(heads, 1, 128), wide(ns, 1, 128), wide(1, 128), wide(ng, 1, 128),
            wide(ns, 1, 128), wide(heads, 1, 128), wide(ns, 128),
            wide(ns, 128), wide(ns, 128), wide(ns, 128), wide(ns, 128),
            wide(heads, ns, 128), wide(heads, ns, 128), wide(heads, ns, 128), wide(heads, ns, 128),
            wide(ng, 128), wide(ng, 128), wide(heads, ng, 128), wide(heads, ng, 128),
            dma((5,)),
            dma((len(SIZES),)), dma((len(SIZES),)), dma((1,)), dma((1,)),
            dma((len(SIZES), ng)), dma((len(SIZES), ng)), dma((ng,)), dma((ng,)),
            dma((len(SIZES),)), dma((len(SIZES),)), dma((1,)), dma((heads,)),
            dma((heads,)), dma((1,)), dma((ng,)), dma((ng,)),
        ],
        compiler_params=pltpu.CompilerParams(collective_id=0, has_side_effects=True),
        name="mlstm_layer",
    )(queries, key_vectors, value_vectors, input_gate, forget_gate)


def solution(mesh):
    return jax.shard_map(
        functools.partial(on_device, mesh.shape["grp"], mesh.shape["seq"]),
        mesh=mesh,
        in_specs=(
            P(("grp", "seq"), None),
            P(("grp", "seq"), None),
            P(("grp", "seq"), None),
            P(None, ("grp", "seq")),
            P(None, ("grp", "seq")),
        ),
        out_specs=P(("grp", "seq"), None),
        check_vma=False,
    )
```

```python
import functools

import jax
import jax.numpy as jnp
from jax import lax
from jax.experimental import pallas as pl
from jax.experimental.pallas import tpu as pltpu
from jax.sharding import PartitionSpec as P

MESH = pl.DeviceIdType.MESH
FLOOR = -1e30
SIZES = (1, 1, 1, 1)
COLUMNS = (0, 1, 2, 3, 4, 7, 5, 6)


def split3(x):
    hi = x.astype(jnp.bfloat16)
    rest = x - hi.astype(jnp.float32)
    mid = rest.astype(jnp.bfloat16)
    low = (rest - mid.astype(jnp.float32)).astype(jnp.bfloat16)
    return hi, mid, low


def kernel(
    ng, ns, heads, kd, vd, length,
    q_hbm, k_hbm, v_hbm, ig_hbm, fg_hbm, o_ref,
    ig, fg, qv, kv, vv, state, inner, rbuf, pbuf, pfull, gsend, grecv,
    small, rsmall, gsmall, grsmall, vec, rvec, gvec, grvec, nback, rnback, nrows,
    rows_a, rows_b, rows_t, rows_d, wide_a, wide_b, wide_c, wide_d, group_a, group_b, group_wide_a, group_wide_b,
    in_sem, s1, r1, ss, rs, sg, rg, sgs, rgs, s3, r3, sn, rn, sv, rv, sgv, rgv,
):
    f32, bf16 = jnp.float32, jnp.bfloat16
    chunks = len(SIZES)
    first = [sum(SIZES[:c]) for c in range(chunks + 1)]
    rp = kd * (vd // 128) // ns
    cols = vd // 128
    per_head = ns // heads
    span = 64 // heads
    scale = kd ** (-0.5)
    myg = lax.axis_index("grp")
    me = lax.axis_index("seq")
    myh = me // per_head
    owns_vector = (me & (per_head - 1)) == 0

    def seq_peer(d):
        return (me + d) & (ns - 1)

    def grp_peer(d):
        return (myg + d) & (ng - 1)

    zdim = min(8, ns)
    ydim = ns // zdim
    zbits = zdim.bit_length() - 1
    y, z = me >> zbits, me & (zdim - 1)

    def each_peer(do):
        for d in range(1, ns):
            do(seq_peer(d))

    def far_first(do):
        def far(n, size):
            return min(n, size - n)

        steps = [(dy, dz) for dy in range(ydim) for dz in range(zdim) if dy or dz]
        steps.sort(key=lambda t: (far(t[1], zdim), far(t[0], ydim)), reverse=True)
        for dy, dz in steps:
            do((((y + dy) & (ydim - 1)) << zbits) | ((z + dz) & (zdim - 1)))

    def to_columns(do, columns):
        for to in columns:
            for dy in range(ydim):
                o = (((y + dy) & (ydim - 1)) << zbits) | to
                if dy:
                    do(o)
                else:
                    pl.when(to != z)(functools.partial(do, o))

    copies = [
        pltpu.make_async_copy(src, dst, in_sem.at[n])
        for n, (src, dst) in enumerate(
            ((fg_hbm, fg), (ig_hbm, ig), (k_hbm, kv), (v_hbm, vv), (q_hbm, qv))
        )
    ]
    for copy in copies:
        copy.start()

    barrier = pltpu.get_barrier_semaphore()

    def greet(device):
        pl.semaphore_signal(barrier, inc=1, device_id=device, device_id_type=MESH)

    each_peer(lambda o: greet((myg, o)))
    for d in range(1, ng):
        greet((grp_peer(d), me))

    zero = jnp.zeros((1, 128), f32)

    @pl.loop(myg + 1, ng)
    def _(g):
        grsmall[g] = zero
        grvec[g] = zero
        for h in range(heads):
            grecv[g, h] = jnp.zeros((rp, 128), f32)

    lane = lax.broadcasted_iota(jnp.int32, (heads, 128), 1)
    head_row = lax.broadcasted_iota(jnp.int32, (heads, 128), 0)
    rows = lax.broadcasted_iota(jnp.int32, (length, length), 0)
    lanes = lax.broadcasted_iota(jnp.int32, (length, length), 1)

    def slice_of(ref, c, o):
        row = pl.multiple_of((o >> (cols.bit_length() - 1)) * rp, 8)
        col = pl.multiple_of((o & (cols - 1)) * 128, 128)
        return ref.at[pl.ds(first[c], SIZES[c]), pl.ds(row, rp), pl.ds(col, 128)]

    def part(c):
        return pl.ds(first[c], SIZES[c])

    def remote(src, dst, send, recv, device):
        return pltpu.make_async_remote_copy(
            src_ref=src, dst_ref=dst, send_sem=send, recv_sem=recv, device_id=device, device_id_type=MESH
        )

    def small_copy(o, slot):
        return remote(
            small, rsmall.at[slot], ss.at[0], rs.at[0], (myg, o)
        )

    def block_vector_copy(h, o, slot):
        return remote(vec.at[h], rvec.at[slot], sv.at[h], rv.at[0], (myg, o))

    def group_vector_copy(o, slot):
        return remote(gvec, grvec.at[slot], sgv.at[o], rgv.at[slot], (o, me))

    def state_copy(c, o, slot):
        return remote(
            slice_of(state, c, o), rbuf.at[slot, part(c)], s1.at[c], r1.at[c], (myg, o)
        )

    def back_copy(c, o, slot):
        return remote(
            pbuf.at[o, part(c)], slice_of(pfull, c, slot), s3.at[c], r3.at[c], (myg, o)
        )

    def vector_copy(o, h):
        return remote(nback.at[o], rnback.at[h], sn.at[0], rn.at[h], (myg, o))

    others = pl.ds(0, ns - 1)

    def all_small():
        return remote(rsmall.at[others], rsmall.at[others], ss.at[0], rs.at[0], (myg, me))

    def all_state(c):
        ref = rbuf.at[others, part(c)]
        return remote(ref, ref, s1.at[c], r1.at[c], (myg, me))

    def all_back(c):
        ref = pbuf.at[others, part(c)]
        return remote(ref, ref, s3.at[c], r3.at[c], (myg, me))

    def all_block_vectors():
        return remote(rvec.at[others], rvec.at[others], sv.at[0], rv.at[0], (myg, me))

    def all_vectors():
        return remote(nback.at[others], nback.at[others], sn.at[0], rn.at[0], (myg, me))

    def group_small_copy(o, slot):
        return remote(gsmall, grsmall.at[slot], sgs.at[o], rgs.at[slot], (o, me))

    def group_copy(c, o, slot):
        return remote(
            gsend.at[part(c)], grecv.at[slot, part(c)], sg.at[c, o], rg.at[c, slot], (o, me)
        )

    upper = jnp.where(rows <= lanes, 1.0, 0.0).astype(bf16)
    copies[0].wait()
    copies[1].wait()
    forget = fg[...]
    logf = jnp.minimum(forget, 0.0) - jnp.log1p(jnp.exp(-jnp.abs(forget)))

    def exact_rows(values, matrix):
        hi, mid, low = split3(values)
        lhs = jnp.concatenate([hi, mid, low, jnp.zeros_like(low)], axis=0)
        out = jnp.dot(lhs, matrix, preferred_element_type=f32)
        n = values.shape[0]
        return out[0:n] + out[n : 2 * n] + out[2 * n : 3 * n]

    cumul = exact_rows(logf, upper)
    level = ig[...] - cumul
    decay = cumul[:, length - 1 : length]
    level_top = jnp.max(level, axis=1, keepdims=True)
    weight = jnp.exp(level - level_top)
    top = decay + level_top

    mine = jnp.where(lane < 64, decay, top)
    pick = lax.div(lax.rem(lane, 64), span) == head_row
    scalars = jnp.sum(jnp.where(pick, mine, 0.0), axis=0, keepdims=True)

    copies[2].wait()
    copies[3].wait()

    def local_state(c):
        for h in range(first[c], first[c + 1]):
            turned = kv[:, h * kd : (h + 1) * kd].astype(f32).T
            scaled = (turned * weight[h : h + 1, :]).astype(bf16)
            state[h] = jnp.dot(scaled, vv[:, h * vd : (h + 1) * vd], preferred_element_type=f32)
        rbuf[me, first[c] : first[c + 1]] = slice_of(state, c, me)[...]

    def send_state(c):
        far_first(lambda o: state_copy(c, o, me).start())

    small[...] = scalars
    rsmall[me] = scalars
    local_state(0)
    pl.semaphore_wait(barrier, ns - 1 + ng - 1)

    each_peer(lambda o: small_copy(o, me).start())

    send_state(0)
    for c in range(1, chunks):
        local_state(c)
        send_state(c)

    for h in range(heads):
        vector = exact_rows(weight, kv[:, h * kd : (h + 1) * kd])
        vec[h] = vector[h : h + 1, :]
    for h in range(heads):
        @pl.when(me == h * per_head)
        def _(h=h):
            rvec[me] = vec[h]

        @pl.when(me != h * per_head)
        def _(h=h):
            block_vector_copy(h, h * per_head, me).start()

    copies[4].wait()
    columns = []
    for h in range(heads):
        scores = scale * lax.dot_general(
            qv[:, h * kd : (h + 1) * kd], kv[:, h * kd : (h + 1) * kd],
            (((1,), (1,)), ((), ())), preferred_element_type=f32,
        )
        masked = jnp.where(rows >= lanes, level[h : h + 1, :], -jnp.inf)
        reach = jnp.max(masked, axis=1, keepdims=True)
        weighted = jnp.exp(masked - reach) * scores
        inner_den = jnp.sum(weighted, axis=1, keepdims=True)
        cumul_col = jnp.sum(
            jnp.where(rows == lanes, cumul[h : h + 1, :], 0.0), axis=1, keepdims=True
        )
        inner[h] = jnp.dot(
            weighted.astype(bf16), vv[:, h * vd : (h + 1) * vd], preferred_element_type=f32
        )
        columns.append((reach, inner_den, cumul_col))

    all_small().wait_recv()

    def widen(out, source):
        for h in range(heads):
            out[h] = jnp.broadcast_to(source[:, h * span : h * span + 1], (ns, 128))

    run_top = jnp.full((1, 128), FLOOR, f32)
    run_dec = jnp.zeros((1, 128), f32)
    for i in range(ns):
        row = rsmall[i]
        top_i = pltpu.roll(row, 64, 1)
        rows_t[i : i + 1, :] = run_top
        rows_d[i : i + 1, :] = run_dec
        early = run_top + row
        joined = jnp.maximum(early, top_i)
        rows_a[i : i + 1, :] = early - joined
        rows_b[i : i + 1, :] = top_i - joined
        run_top = joined
        run_dec = run_dec + row
    lane1 = lax.broadcasted_iota(jnp.int32, (1, 128), 1)
    widen(wide_a, jnp.exp(rows_a[...]))
    widen(wide_b, jnp.exp(rows_b[...]))

    total = jnp.where(lane1 < 64, run_dec, pltpu.roll(run_top, 64, 1))
    gsmall[...] = total
    grsmall[myg] = total

    @pl.loop(myg + 1, ng)
    def _(d):
        group_small_copy(d, myg).start()

    def scan_vector():
        @pl.when(owns_vector)
        def _():
            all_block_vectors().wait_recv()

            run_vec = jnp.zeros((1, 128), f32)
            for i in range(ns):
                nrows[i : i + 1, :] = run_vec
                run_vec = wide_a[myh, i : i + 1, :] * run_vec + wide_b[myh, i : i + 1, :] * rvec[i]
            gvec[...] = run_vec
            grvec[myg] = run_vec

            @pl.loop(myg + 1, ng)
            def _(d):
                group_vector_copy(d, myg).start()

    def scan(c):
        all_state(c).wait_recv()

        for h in range(first[c], first[c + 1]):
            run = jnp.zeros((rp, 128), f32)
            for i in range(ns):
                pbuf[i, h] = run
                run = wide_a[h, i : i + 1, :] * run + wide_b[h, i : i + 1, :] * rbuf[i, h]
            gsend[h] = run
        grecv[myg, first[c] : first[c + 1]] = gsend[first[c] : first[c + 1]]

        @pl.loop(myg + 1, ng)
        def _(d):
            group_copy(c, d, myg).start()

    order = [(what, c) for c in range(chunks) for what in ("scan", "back")]
    order = order[:1] + [("group", 0)] + order[1:-1] + [("vector", 0)] + order[-1:] + [("return", 0)]

    found = []

    def before_group():
        @pl.loop(0, myg)
        def _(d):
            o = d
            group_small_copy(o, o).wait_recv()

        before_top = jnp.full((1, 128), FLOOR, f32)
        for g in range(ng):
            row = grsmall[g]
            top_g = pltpu.roll(row, 64, 1)
            counts = g < myg
            early = before_top + row
            joined = jnp.maximum(early, top_g)
            a = jnp.where(counts, jnp.exp(early - joined), 1.0)
            b = jnp.where(counts, jnp.exp(top_g - joined), 0.0)
            before_top = jnp.where(counts, joined, before_top)
            group_a[g : g + 1, :] = a
            group_b[g : g + 1, :] = b
        tops = rows_t[...]
        early = before_top + rows_d[...]
        full = jnp.maximum(early, tops)
        rows_t[...] = full
        found.append(rows_t[pl.ds(me, 1), :])
        widen(wide_c, jnp.exp(early - full))
        widen(wide_d, jnp.exp(tops - full))
        for h in range(heads):
            group_wide_a[h] = jnp.broadcast_to(group_a[:, h * span : h * span + 1], (ng, 128))
            group_wide_b[h] = jnp.broadcast_to(group_b[:, h * span : h * span + 1], (ng, 128))

    def return_vector():
        @pl.when(owns_vector)
        def _():
            @pl.loop(0, myg)
            def _(d):
                o = d
                group_vector_copy(o, o).wait_recv()

            before = jnp.zeros((1, 128), f32)
            for g in range(ng):
                before = (
                    group_wide_a[myh, g : g + 1, :] * before
                    + group_wide_b[myh, g : g + 1, :] * grvec[g]
                )
            vectors = wide_c[myh] * before + wide_d[myh] * nrows[...]
            for i in range(ns):
                nback[i] = vectors[i : i + 1, :]
            rnback[myh] = nback[me]

            @pl.loop(1, ns)
            def _(d):
                vector_copy(seq_peer(d), myh).start()

    def back(c):
        @pl.loop(0, myg)
        def _(d):
            o = d
            group_copy(c, o, o).wait_recv()

        for h in range(first[c], first[c + 1]):
            run = jnp.zeros((rp, 128), f32)
            for g in range(ng):
                run = group_wide_a[h, g : g + 1, :] * run + group_wide_b[h, g : g + 1, :] * grecv[g, h]
            for i in range(ns):
                pbuf[i, h] = wide_c[h, i : i + 1, :] * run + wide_d[h, i : i + 1, :] * pbuf[i, h]

        to_columns(lambda o: back_copy(c, o, me).start(), COLUMNS)
        slice_of(pfull, c, me)[...] = pbuf[me, first[c] : first[c + 1]]

    for what, c in order:
        if what == "scan":
            scan(c)
        elif what == "back":
            back(c)
        elif what == "group":
            before_group()
        elif what == "vector":
            scan_vector()
        else:
            return_vector()

    for h in range(heads):
        @pl.when(me != h * per_head)
        def _(h=h):
            vector_copy(h * per_head, h).wait_recv()

    for c in range(chunks):
        all_back(c).wait_recv()

        for h in range(first[c], first[c + 1]):
            reach, inner_den, cumul_col = columns[h]
            query = qv[:, h * kd : (h + 1) * kd]
            carried = scale * jnp.dot(query, pfull[h].astype(bf16), preferred_element_type=f32)
            carried_den = scale * jnp.sum(query.astype(f32) * rnback[h], axis=1, keepdims=True)
            prev = found[0][:, h * span : h * span + 1]
            peak = jnp.maximum(prev, reach)
            inner_factor = jnp.exp(reach - peak)
            outer_factor = jnp.exp(prev - peak)
            denom = inner_factor * inner_den + outer_factor * carried_den
            bound = jnp.maximum(jnp.abs(denom), jnp.exp(-(cumul_col + peak)))
            numer = inner_factor * inner[h] + outer_factor * carried
            o_ref[:, h * vd : (h + 1) * vd] = (numer / bound).astype(bf16)

    all_small().wait_send()
    for c in range(chunks):
        all_state(c).wait_send()
        all_back(c).wait_send()

    for h in range(heads):
        @pl.when(me != h * per_head)
        def _(h=h):
            block_vector_copy(h, h * per_head, me).wait_send()

    @pl.when(owns_vector)
    def _():
        all_vectors().wait_send()

        @pl.loop(myg + 1, ng)
        def _(d):
            group_vector_copy(d, myg).wait_send()

    @pl.loop(myg + 1, ng)
    def _(d):
        o = d
        group_small_copy(o, myg).wait_send()
        for c in range(chunks):
            group_copy(c, o, myg).wait_send()


def on_device(ng, ns, queries, key_vectors, value_vectors, input_gate, forget_gate):
    heads, length = input_gate.shape
    kd = queries.shape[1] // heads
    vd = value_vectors.shape[1] // heads
    rp = kd * (vd // 128) // ns
    dma = pltpu.SemaphoreType.DMA

    def wide(*shape):
        return pltpu.VMEM(shape, jnp.float32)

    return pl.pallas_call(
        functools.partial(kernel, ng, ns, heads, kd, vd, length),
        out_shape=pltpu.VMEM(value_vectors.shape, jnp.bfloat16),
        in_specs=[pl.BlockSpec(memory_space=pl.ANY)] * 5,
        out_specs=pl.BlockSpec(memory_space=pltpu.VMEM),
        scratch_shapes=[
            wide(heads, length), wide(heads, length),
            pltpu.VMEM(queries.shape, jnp.bfloat16),
            pltpu.VMEM(key_vectors.shape, jnp.bfloat16),
            pltpu.VMEM(value_vectors.shape, jnp.bfloat16),
            wide(heads, kd, vd), wide(heads, length, vd),
            wide(ns, heads, rp, 128), wide(ns, heads, rp, 128), wide(heads, kd, vd),
            wide(heads, rp, 128), wide(ng, heads, rp, 128),
            wide(1, 128), wide(ns, 1, 128), wide(1, 128), wide(ng, 1, 128),
            wide(heads, 1, 128), wide(ns, 1, 128), wide(1, 128), wide(ng, 1, 128),
            wide(ns, 1, 128), wide(heads, 1, 128), wide(ns, 128),
            wide(ns, 128), wide(ns, 128), wide(ns, 128), wide(ns, 128),
            wide(heads, ns, 128), wide(heads, ns, 128), wide(heads, ns, 128), wide(heads, ns, 128),
            wide(ng, 128), wide(ng, 128), wide(heads, ng, 128), wide(heads, ng, 128),
            dma((5,)),
            dma((len(SIZES),)), dma((len(SIZES),)), dma((1,)), dma((1,)),
            dma((len(SIZES), ng)), dma((len(SIZES), ng)), dma((ng,)), dma((ng,)),
            dma((len(SIZES),)), dma((len(SIZES),)), dma((1,)), dma((heads,)),
            dma((heads,)), dma((1,)), dma((ng,)), dma((ng,)),
        ],
        compiler_params=pltpu.CompilerParams(collective_id=0, has_side_effects=True),
        name="mlstm_layer",
    )(queries, key_vectors, value_vectors, input_gate, forget_gate)


def solution(mesh):
    return jax.shard_map(
        functools.partial(on_device, mesh.shape["grp"], mesh.shape["seq"]),
        mesh=mesh,
        in_specs=(
            P(("grp", "seq"), None),
            P(("grp", "seq"), None),
            P(("grp", "seq"), None),
            P(None, ("grp", "seq")),
            P(None, ("grp", "seq")),
        ),
        out_specs=P(("grp", "seq"), None),
        check_vma=False,
    )
```

```python
import functools

import jax
import jax.numpy as jnp
from jax import lax
from jax.experimental import pallas as pl
from jax.experimental.pallas import tpu as pltpu
from jax.sharding import PartitionSpec as P

MESH = pl.DeviceIdType.MESH
FLOOR = -1e30
SIZES = (1, 1, 1, 1)
COLUMNS = (0, 1, 2, 3, 4, 7, 5, 6)


def split3(x):
    hi = x.astype(jnp.bfloat16)
    rest = x - hi.astype(jnp.float32)
    mid = rest.astype(jnp.bfloat16)
    low = (rest - mid.astype(jnp.float32)).astype(jnp.bfloat16)
    return hi, mid, low


def kernel(
    ng, ns, heads, kd, vd, length,
    q_hbm, k_hbm, v_hbm, ig_hbm, fg_hbm, o_ref,
    ig, fg, qv, kv, vv, state, inner, rbuf, pbuf, pfull, gsend, grecv,
    small, rsmall, gsmall, grsmall, vec, rvec, gvec, grvec, nback, rnback, nrows,
    rows_a, rows_b, rows_t, rows_d, wide_a, wide_b, wide_c, wide_d, group_a, group_b, group_wide_a, group_wide_b,
    in_sem, s1, r1, ss, rs, sg, rg, sgs, rgs, s3, r3, sn, rn, sv, rv, sgv, rgv,
):
    f32, bf16 = jnp.float32, jnp.bfloat16
    chunks = len(SIZES)
    first = [sum(SIZES[:c]) for c in range(chunks + 1)]
    rp = kd * (vd // 128) // ns
    cols = vd // 128
    per_head = ns // heads
    span = 64 // heads
    scale = kd ** (-0.5)
    myg = lax.axis_index("grp")
    me = lax.axis_index("seq")
    myh = me // per_head
    owns_vector = (me & (per_head - 1)) == 0

    def seq_peer(d):
        return (me + d) & (ns - 1)

    def grp_peer(d):
        return (myg + d) & (ng - 1)

    zdim = min(8, ns)
    ydim = ns // zdim
    zbits = zdim.bit_length() - 1
    y, z = me >> zbits, me & (zdim - 1)

    def each_peer(do):
        for d in range(1, ns):
            do(seq_peer(d))

    def far_first(do):
        def far(n, size):
            return min(n, size - n)

        steps = [(dy, dz) for dy in range(ydim) for dz in range(zdim) if dy or dz]
        steps.sort(key=lambda t: (far(t[1], zdim), far(t[0], ydim)), reverse=True)
        for dy, dz in steps:
            do((((y + dy) & (ydim - 1)) << zbits) | ((z + dz) & (zdim - 1)))

    def to_columns(do, columns):
        for low in range(0, ydim, 2):
            for to in columns:
                for k in range(min(2, ydim)):
                    o = ((low + ((y + k) & (min(2, ydim) - 1))) << zbits) | to
                    pl.when(o != me)(functools.partial(do, o))

    copies = [
        pltpu.make_async_copy(src, dst, in_sem.at[n])
        for n, (src, dst) in enumerate(
            ((fg_hbm, fg), (ig_hbm, ig), (k_hbm, kv), (v_hbm, vv), (q_hbm, qv))
        )
    ]
    for copy in copies:
        copy.start()

    barrier = pltpu.get_barrier_semaphore()

    def greet(device):
        pl.semaphore_signal(barrier, inc=1, device_id=device, device_id_type=MESH)

    each_peer(lambda o: greet((myg, o)))
    for d in range(1, ng):
        greet((grp_peer(d), me))

    zero = jnp.zeros((1, 128), f32)

    @pl.loop(myg + 1, ng)
    def _(g):
        grsmall[g] = zero
        grvec[g] = zero
        for h in range(heads):
            grecv[g, h] = jnp.zeros((rp, 128), f32)

    lane = lax.broadcasted_iota(jnp.int32, (heads, 128), 1)
    head_row = lax.broadcasted_iota(jnp.int32, (heads, 128), 0)
    rows = lax.broadcasted_iota(jnp.int32, (length, length), 0)
    lanes = lax.broadcasted_iota(jnp.int32, (length, length), 1)

    def slice_of(ref, c, o):
        row = pl.multiple_of((o >> (cols.bit_length() - 1)) * rp, 8)
        col = pl.multiple_of((o & (cols - 1)) * 128, 128)
        return ref.at[pl.ds(first[c], SIZES[c]), pl.ds(row, rp), pl.ds(col, 128)]

    def part(c):
        return pl.ds(first[c], SIZES[c])

    def remote(src, dst, send, recv, device):
        return pltpu.make_async_remote_copy(
            src_ref=src, dst_ref=dst, send_sem=send, recv_sem=recv, device_id=device, device_id_type=MESH
        )

    def small_copy(o, slot):
        return remote(
            small, rsmall.at[slot], ss.at[0], rs.at[0], (myg, o)
        )

    def block_vector_copy(h, o, slot):
        return remote(vec.at[h], rvec.at[slot], sv.at[h], rv.at[0], (myg, o))

    def group_vector_copy(o, slot):
        return remote(gvec, grvec.at[slot], sgv.at[o], rgv.at[slot], (o, me))

    def state_copy(c, o, slot):
        return remote(
            slice_of(state, c, o), rbuf.at[slot, part(c)], s1.at[c], r1.at[c], (myg, o)
        )

    def back_copy(c, o, slot):
        return remote(
            pbuf.at[o, part(c)], slice_of(pfull, c, slot), s3.at[c], r3.at[c], (myg, o)
        )

    def vector_copy(o, h):
        return remote(nback.at[o], rnback.at[h], sn.at[0], rn.at[h], (myg, o))

    others = pl.ds(0, ns - 1)

    def all_small():
        return remote(rsmall.at[others], rsmall.at[others], ss.at[0], rs.at[0], (myg, me))

    def all_state(c):
        ref = rbuf.at[others, part(c)]
        return remote(ref, ref, s1.at[c], r1.at[c], (myg, me))

    def all_back(c):
        ref = pbuf.at[others, part(c)]
        return remote(ref, ref, s3.at[c], r3.at[c], (myg, me))

    def all_block_vectors():
        return remote(rvec.at[others], rvec.at[others], sv.at[0], rv.at[0], (myg, me))

    def all_vectors():
        return remote(nback.at[others], nback.at[others], sn.at[0], rn.at[0], (myg, me))

    def group_small_copy(o, slot):
        return remote(gsmall, grsmall.at[slot], sgs.at[o], rgs.at[slot], (o, me))

    def group_copy(c, o, slot):
        return remote(
            gsend.at[part(c)], grecv.at[slot, part(c)], sg.at[c, o], rg.at[c, slot], (o, me)
        )

    upper = jnp.where(rows <= lanes, 1.0, 0.0).astype(bf16)
    copies[0].wait()
    copies[1].wait()
    forget = fg[...]
    logf = jnp.minimum(forget, 0.0) - jnp.log1p(jnp.exp(-jnp.abs(forget)))

    def exact_rows(values, matrix):
        hi, mid, low = split3(values)
        lhs = jnp.concatenate([hi, mid, low, jnp.zeros_like(low)], axis=0)
        out = jnp.dot(lhs, matrix, preferred_element_type=f32)
        n = values.shape[0]
        return out[0:n] + out[n : 2 * n] + out[2 * n : 3 * n]

    cumul = exact_rows(logf, upper)
    level = ig[...] - cumul
    decay = cumul[:, length - 1 : length]
    level_top = jnp.max(level, axis=1, keepdims=True)
    weight = jnp.exp(level - level_top)
    top = decay + level_top

    mine = jnp.where(lane < 64, decay, top)
    pick = lax.div(lax.rem(lane, 64), span) == head_row
    scalars = jnp.sum(jnp.where(pick, mine, 0.0), axis=0, keepdims=True)

    copies[2].wait()
    copies[3].wait()

    def local_state(c):
        for h in range(first[c], first[c + 1]):
            turned = kv[:, h * kd : (h + 1) * kd].astype(f32).T
            scaled = (turned * weight[h : h + 1, :]).astype(bf16)
            state[h] = jnp.dot(scaled, vv[:, h * vd : (h + 1) * vd], preferred_element_type=f32)
        rbuf[me, first[c] : first[c + 1]] = slice_of(state, c, me)[...]

    def send_state(c):
        far_first(lambda o: state_copy(c, o, me).start())

    small[...] = scalars
    rsmall[me] = scalars
    local_state(0)
    pl.semaphore_wait(barrier, ns - 1 + ng - 1)

    each_peer(lambda o: small_copy(o, me).start())

    send_state(0)
    for c in range(1, chunks):
        local_state(c)
        send_state(c)

    for h in range(heads):
        vector = exact_rows(weight, kv[:, h * kd : (h + 1) * kd])
        vec[h] = vector[h : h + 1, :]
    for h in range(heads):
        @pl.when(me == h * per_head)
        def _(h=h):
            rvec[me] = vec[h]

        @pl.when(me != h * per_head)
        def _(h=h):
            block_vector_copy(h, h * per_head, me).start()

    copies[4].wait()
    columns = []
    for h in range(heads):
        scores = scale * lax.dot_general(
            qv[:, h * kd : (h + 1) * kd], kv[:, h * kd : (h + 1) * kd],
            (((1,), (1,)), ((), ())), preferred_element_type=f32,
        )
        masked = jnp.where(rows >= lanes, level[h : h + 1, :], -jnp.inf)
        reach = jnp.max(masked, axis=1, keepdims=True)
        weighted = jnp.exp(masked - reach) * scores
        inner_den = jnp.sum(weighted, axis=1, keepdims=True)
        cumul_col = jnp.sum(
            jnp.where(rows == lanes, cumul[h : h + 1, :], 0.0), axis=1, keepdims=True
        )
        inner[h] = jnp.dot(
            weighted.astype(bf16), vv[:, h * vd : (h + 1) * vd], preferred_element_type=f32
        )
        columns.append((reach, inner_den, cumul_col))

    all_small().wait_recv()

    def widen(out, source):
        for h in range(heads):
            out[h] = jnp.broadcast_to(source[:, h * span : h * span + 1], (ns, 128))

    run_top = jnp.full((1, 128), FLOOR, f32)
    run_dec = jnp.zeros((1, 128), f32)
    for i in range(ns):
        row = rsmall[i]
        top_i = pltpu.roll(row, 64, 1)
        rows_t[i : i + 1, :] = run_top
        rows_d[i : i + 1, :] = run_dec
        early = run_top + row
        joined = jnp.maximum(early, top_i)
        rows_a[i : i + 1, :] = early - joined
        rows_b[i : i + 1, :] = top_i - joined
        run_top = joined
        run_dec = run_dec + row
    lane1 = lax.broadcasted_iota(jnp.int32, (1, 128), 1)
    widen(wide_a, jnp.exp(rows_a[...]))
    widen(wide_b, jnp.exp(rows_b[...]))

    total = jnp.where(lane1 < 64, run_dec, pltpu.roll(run_top, 64, 1))
    gsmall[...] = total
    grsmall[myg] = total

    @pl.loop(myg + 1, ng)
    def _(d):
        group_small_copy(d, myg).start()

    def scan_vector():
        @pl.when(owns_vector)
        def _():
            all_block_vectors().wait_recv()

            run_vec = jnp.zeros((1, 128), f32)
            for i in range(ns):
                nrows[i : i + 1, :] = run_vec
                run_vec = wide_a[myh, i : i + 1, :] * run_vec + wide_b[myh, i : i + 1, :] * rvec[i]
            gvec[...] = run_vec
            grvec[myg] = run_vec

            @pl.loop(myg + 1, ng)
            def _(d):
                group_vector_copy(d, myg).start()

    def scan(c):
        all_state(c).wait_recv()

        for h in range(first[c], first[c + 1]):
            run = jnp.zeros((rp, 128), f32)
            for i in range(ns):
                pbuf[i, h] = run
                run = wide_a[h, i : i + 1, :] * run + wide_b[h, i : i + 1, :] * rbuf[i, h]
            gsend[h] = run
        grecv[myg, first[c] : first[c + 1]] = gsend[first[c] : first[c + 1]]

        @pl.loop(myg + 1, ng)
        def _(d):
            group_copy(c, d, myg).start()

    order = [(what, c) for c in range(chunks) for what in ("scan", "back")]
    order = order[:1] + [("group", 0)] + order[1:-1] + [("vector", 0)] + order[-1:] + [("return", 0)]

    found = []

    def before_group():
        @pl.loop(0, myg)
        def _(d):
            o = d
            group_small_copy(o, o).wait_recv()

        before_top = jnp.full((1, 128), FLOOR, f32)
        for g in range(ng):
            row = grsmall[g]
            top_g = pltpu.roll(row, 64, 1)
            counts = g < myg
            early = before_top + row
            joined = jnp.maximum(early, top_g)
            a = jnp.where(counts, jnp.exp(early - joined), 1.0)
            b = jnp.where(counts, jnp.exp(top_g - joined), 0.0)
            before_top = jnp.where(counts, joined, before_top)
            group_a[g : g + 1, :] = a
            group_b[g : g + 1, :] = b
        tops = rows_t[...]
        early = before_top + rows_d[...]
        full = jnp.maximum(early, tops)
        rows_t[...] = full
        found.append(rows_t[pl.ds(me, 1), :])
        widen(wide_c, jnp.exp(early - full))
        widen(wide_d, jnp.exp(tops - full))
        for h in range(heads):
            group_wide_a[h] = jnp.broadcast_to(group_a[:, h * span : h * span + 1], (ng, 128))
            group_wide_b[h] = jnp.broadcast_to(group_b[:, h * span : h * span + 1], (ng, 128))

    def return_vector():
        @pl.when(owns_vector)
        def _():
            @pl.loop(0, myg)
            def _(d):
                o = d
                group_vector_copy(o, o).wait_recv()

            before = jnp.zeros((1, 128), f32)
            for g in range(ng):
                before = (
                    group_wide_a[myh, g : g + 1, :] * before
                    + group_wide_b[myh, g : g + 1, :] * grvec[g]
                )
            vectors = wide_c[myh] * before + wide_d[myh] * nrows[...]
            for i in range(ns):
                nback[i] = vectors[i : i + 1, :]
            rnback[myh] = nback[me]

            @pl.loop(1, ns)
            def _(d):
                vector_copy(seq_peer(d), myh).start()

    def back(c):
        @pl.loop(0, myg)
        def _(d):
            o = d
            group_copy(c, o, o).wait_recv()

        for h in range(first[c], first[c + 1]):
            run = jnp.zeros((rp, 128), f32)
            for g in range(ng):
                run = group_wide_a[h, g : g + 1, :] * run + group_wide_b[h, g : g + 1, :] * grecv[g, h]
            for i in range(ns):
                pbuf[i, h] = wide_c[h, i : i + 1, :] * run + wide_d[h, i : i + 1, :] * pbuf[i, h]

        to_columns(lambda o: back_copy(c, o, me).start(), COLUMNS)
        slice_of(pfull, c, me)[...] = pbuf[me, first[c] : first[c + 1]]

    for what, c in order:
        if what == "scan":
            scan(c)
        elif what == "back":
            back(c)
        elif what == "group":
            before_group()
        elif what == "vector":
            scan_vector()
        else:
            return_vector()

    for h in range(heads):
        @pl.when(me != h * per_head)
        def _(h=h):
            vector_copy(h * per_head, h).wait_recv()

    for c in range(chunks):
        all_back(c).wait_recv()

        for h in range(first[c], first[c + 1]):
            reach, inner_den, cumul_col = columns[h]
            query = qv[:, h * kd : (h + 1) * kd]
            carried = scale * jnp.dot(query, pfull[h].astype(bf16), preferred_element_type=f32)
            carried_den = scale * jnp.sum(query.astype(f32) * rnback[h], axis=1, keepdims=True)
            prev = found[0][:, h * span : h * span + 1]
            peak = jnp.maximum(prev, reach)
            inner_factor = jnp.exp(reach - peak)
            outer_factor = jnp.exp(prev - peak)
            denom = inner_factor * inner_den + outer_factor * carried_den
            bound = jnp.maximum(jnp.abs(denom), jnp.exp(-(cumul_col + peak)))
            numer = inner_factor * inner[h] + outer_factor * carried
            o_ref[:, h * vd : (h + 1) * vd] = (numer / bound).astype(bf16)

    all_small().wait_send()
    for c in range(chunks):
        all_state(c).wait_send()
        all_back(c).wait_send()

    for h in range(heads):
        @pl.when(me != h * per_head)
        def _(h=h):
            block_vector_copy(h, h * per_head, me).wait_send()

    @pl.when(owns_vector)
    def _():
        all_vectors().wait_send()

        @pl.loop(myg + 1, ng)
        def _(d):
            group_vector_copy(d, myg).wait_send()

    @pl.loop(myg + 1, ng)
    def _(d):
        o = d
        group_small_copy(o, myg).wait_send()
        for c in range(chunks):
            group_copy(c, o, myg).wait_send()


def on_device(ng, ns, queries, key_vectors, value_vectors, input_gate, forget_gate):
    heads, length = input_gate.shape
    kd = queries.shape[1] // heads
    vd = value_vectors.shape[1] // heads
    rp = kd * (vd // 128) // ns
    dma = pltpu.SemaphoreType.DMA

    def wide(*shape):
        return pltpu.VMEM(shape, jnp.float32)

    return pl.pallas_call(
        functools.partial(kernel, ng, ns, heads, kd, vd, length),
        out_shape=pltpu.VMEM(value_vectors.shape, jnp.bfloat16),
        in_specs=[pl.BlockSpec(memory_space=pl.ANY)] * 5,
        out_specs=pl.BlockSpec(memory_space=pltpu.VMEM),
        scratch_shapes=[
            wide(heads, length), wide(heads, length),
            pltpu.VMEM(queries.shape, jnp.bfloat16),
            pltpu.VMEM(key_vectors.shape, jnp.bfloat16),
            pltpu.VMEM(value_vectors.shape, jnp.bfloat16),
            wide(heads, kd, vd), wide(heads, length, vd),
            wide(ns, heads, rp, 128), wide(ns, heads, rp, 128), wide(heads, kd, vd),
            wide(heads, rp, 128), wide(ng, heads, rp, 128),
            wide(1, 128), wide(ns, 1, 128), wide(1, 128), wide(ng, 1, 128),
            wide(heads, 1, 128), wide(ns, 1, 128), wide(1, 128), wide(ng, 1, 128),
            wide(ns, 1, 128), wide(heads, 1, 128), wide(ns, 128),
            wide(ns, 128), wide(ns, 128), wide(ns, 128), wide(ns, 128),
            wide(heads, ns, 128), wide(heads, ns, 128), wide(heads, ns, 128), wide(heads, ns, 128),
            wide(ng, 128), wide(ng, 128), wide(heads, ng, 128), wide(heads, ng, 128),
            dma((5,)),
            dma((len(SIZES),)), dma((len(SIZES),)), dma((1,)), dma((1,)),
            dma((len(SIZES), ng)), dma((len(SIZES), ng)), dma((ng,)), dma((ng,)),
            dma((len(SIZES),)), dma((len(SIZES),)), dma((1,)), dma((heads,)),
            dma((heads,)), dma((1,)), dma((ng,)), dma((ng,)),
        ],
        compiler_params=pltpu.CompilerParams(collective_id=0, has_side_effects=True),
        name="mlstm_layer",
    )(queries, key_vectors, value_vectors, input_gate, forget_gate)


def solution(mesh):
    return jax.shard_map(
        functools.partial(on_device, mesh.shape["grp"], mesh.shape["seq"]),
        mesh=mesh,
        in_specs=(
            P(("grp", "seq"), None),
            P(("grp", "seq"), None),
            P(("grp", "seq"), None),
            P(None, ("grp", "seq")),
            P(None, ("grp", "seq")),
        ),
        out_specs=P(("grp", "seq"), None),
        check_vma=False,
    )
```

```python
import functools

import jax
import jax.numpy as jnp
from jax import lax
from jax.experimental import pallas as pl
from jax.experimental.pallas import tpu as pltpu
from jax.sharding import PartitionSpec as P

MESH = pl.DeviceIdType.MESH
FLOOR = -1e30
SIZES = (1, 1, 1, 1)
RET = 6
COLUMNS = (0, 1, 2, 3, 4, 7, 5, 6)


def split3(x):
    hi = x.astype(jnp.bfloat16)
    rest = x - hi.astype(jnp.float32)
    mid = rest.astype(jnp.bfloat16)
    low = (rest - mid.astype(jnp.float32)).astype(jnp.bfloat16)
    return hi, mid, low


def kernel(
    ng, ns, heads, kd, vd, length,
    q_hbm, k_hbm, v_hbm, ig_hbm, fg_hbm, o_ref,
    ig, fg, qv, kv, vv, state, inner, rbuf, pbuf, pfull, gsend, grecv,
    small, rsmall, gsmall, grsmall, vec, rvec, gvec, grvec, nback, rnback, nrows,
    rows_a, rows_b, rows_t, rows_d, wide_a, wide_b, wide_c, wide_d, group_a, group_b, group_wide_a, group_wide_b,
    in_sem, s1, r1, ss, rs, sg, rg, sgs, rgs, s3, r3, sn, rn, sv, rv, sgv, rgv,
):
    f32, bf16 = jnp.float32, jnp.bfloat16
    chunks = len(SIZES)
    first = [sum(SIZES[:c]) for c in range(chunks + 1)]
    rp = kd * (vd // 128) // ns
    cols = vd // 128
    per_head = ns // heads
    span = 64 // heads
    scale = kd ** (-0.5)
    myg = lax.axis_index("grp")
    me = lax.axis_index("seq")
    myh = me // per_head
    keeper = 0
    owns_vector = (me & (per_head - 1)) == keeper

    def seq_peer(d):
        return (me + d) & (ns - 1)

    def grp_peer(d):
        return (myg + d) & (ng - 1)

    zdim = min(8, ns)
    ydim = ns // zdim
    zbits = zdim.bit_length() - 1
    y, z = me >> zbits, me & (zdim - 1)

    def each_peer(do):
        for d in range(1, ns):
            do(seq_peer(d))

    def far_first(do):
        def far(n, size):
            return min(n, size - n)

        steps = [(dy, dz) for dy in range(ydim) for dz in range(zdim) if dy or dz]
        steps.sort(key=lambda t: (far(t[0], ydim) + far(t[1], zdim)), reverse=True)
        for dy, dz in steps:
            do((((y + dy) & (ydim - 1)) << zbits) | ((z + dz) & (zdim - 1)))

    def to_columns(do, columns):
        for low in range(0, ydim, 2):
            for to in columns:
                for k in range(min(2, ydim)):
                    o = ((low + ((y + k) & (min(2, ydim) - 1))) << zbits) | to
                    pl.when(o != me)(functools.partial(do, o))

    copies = [
        pltpu.make_async_copy(src, dst, in_sem.at[n])
        for n, (src, dst) in enumerate(
            ((fg_hbm, fg), (ig_hbm, ig), (k_hbm, kv), (v_hbm, vv), (q_hbm, qv))
        )
    ]
    for copy in copies:
        copy.start()

    barrier = pltpu.get_barrier_semaphore()

    def greet(device):
        pl.semaphore_signal(barrier, inc=1, device_id=device, device_id_type=MESH)

    each_peer(lambda o: greet((myg, o)))
    for d in range(1, ng):
        greet((grp_peer(d), me))

    zero = jnp.zeros((1, 128), f32)

    @pl.loop(myg + 1, ng)
    def _(g):
        grsmall[g] = zero
        grvec[g] = zero
        for h in range(heads):
            grecv[g, h] = jnp.zeros((rp, 128), f32)

    lane = lax.broadcasted_iota(jnp.int32, (heads, 128), 1)
    head_row = lax.broadcasted_iota(jnp.int32, (heads, 128), 0)
    rows = lax.broadcasted_iota(jnp.int32, (length, length), 0)
    lanes = lax.broadcasted_iota(jnp.int32, (length, length), 1)

    def slice_of(ref, c, o):
        row = pl.multiple_of((o >> (cols.bit_length() - 1)) * rp, 8)
        col = pl.multiple_of((o & (cols - 1)) * 128, 128)
        return ref.at[pl.ds(first[c], SIZES[c]), pl.ds(row, rp), pl.ds(col, 128)]

    def part(c):
        return pl.ds(first[c], SIZES[c])

    def remote(src, dst, send, recv, device):
        return pltpu.make_async_remote_copy(
            src_ref=src, dst_ref=dst, send_sem=send, recv_sem=recv, device_id=device, device_id_type=MESH
        )

    def small_copy(o, slot):
        return remote(
            small, rsmall.at[slot], ss.at[0], rs.at[0], (myg, o)
        )

    def block_vector_copy(h, o, slot):
        return remote(vec.at[h], rvec.at[slot], sv.at[h], rv.at[0], (myg, o))

    def group_vector_copy(o, slot):
        return remote(gvec, grvec.at[slot], sgv.at[o], rgv.at[slot], (o, me))

    def state_copy(c, o, slot):
        return remote(
            slice_of(state, c, o), rbuf.at[slot, part(c)], s1.at[c], r1.at[c], (myg, o)
        )

    def back_copy(c, o, slot):
        return remote(
            pbuf.at[o, part(c)], slice_of(pfull, c, slot), s3.at[c], r3.at[c], (myg, o)
        )

    def vector_copy(o, h):
        return remote(nback.at[o], rnback.at[h], sn.at[0], rn.at[h], (myg, o))

    others = pl.ds(0, ns - 1)

    def all_small():
        return remote(rsmall.at[others], rsmall.at[others], ss.at[0], rs.at[0], (myg, me))

    def all_state(c):
        ref = rbuf.at[others, part(c)]
        return remote(ref, ref, s1.at[c], r1.at[c], (myg, me))

    def all_back(c):
        ref = pbuf.at[others, part(c)]
        return remote(ref, ref, s3.at[c], r3.at[c], (myg, me))

    def all_block_vectors():
        return remote(rvec.at[others], rvec.at[others], sv.at[0], rv.at[0], (myg, me))

    def all_vectors():
        return remote(nback.at[others], nback.at[others], sn.at[0], rn.at[0], (myg, me))

    def group_small_copy(o, slot):
        return remote(gsmall, grsmall.at[slot], sgs.at[o], rgs.at[slot], (o, me))

    def group_copy(c, o, slot):
        return remote(
            gsend.at[part(c)], grecv.at[slot, part(c)], sg.at[c, o], rg.at[c, slot], (o, me)
        )

    upper = jnp.where(rows <= lanes, 1.0, 0.0).astype(bf16)
    copies[0].wait()
    copies[1].wait()
    forget = fg[...]
    logf = jnp.minimum(forget, 0.0) - jnp.log1p(jnp.exp(-jnp.abs(forget)))

    def exact_rows(values, matrix):
        hi, mid, low = split3(values)
        lhs = jnp.concatenate([hi, mid, low, jnp.zeros_like(low)], axis=0)
        out = jnp.dot(lhs, matrix, preferred_element_type=f32)
        n = values.shape[0]
        return out[0:n] + out[n : 2 * n] + out[2 * n : 3 * n]

    cumul = exact_rows(logf, upper)
    level = ig[...] - cumul
    decay = cumul[:, length - 1 : length]
    level_top = jnp.max(level, axis=1, keepdims=True)
    weight = jnp.exp(level - level_top)
    top = decay + level_top

    mine = jnp.where(lane < 64, decay, top)
    pick = lax.div(lax.rem(lane, 64), span) == head_row
    scalars = jnp.sum(jnp.where(pick, mine, 0.0), axis=0, keepdims=True)

    copies[2].wait()
    copies[3].wait()

    def local_state(c):
        for h in range(first[c], first[c + 1]):
            turned = kv[:, h * kd : (h + 1) * kd].astype(f32).T
            scaled = (turned * weight[h : h + 1, :]).astype(bf16)
            state[h] = jnp.dot(scaled, vv[:, h * vd : (h + 1) * vd], preferred_element_type=f32)
        rbuf[me, first[c] : first[c + 1]] = slice_of(state, c, me)[...]

    def send_state(c):
        far_first(lambda o: state_copy(c, o, me).start())

    small[...] = scalars
    rsmall[me] = scalars
    local_state(0)
    pl.semaphore_wait(barrier, ns - 1 + ng - 1)

    each_peer(lambda o: small_copy(o, me).start())

    send_state(0)
    for h in range(heads):
        vector = exact_rows(weight, kv[:, h * kd : (h + 1) * kd])
        vec[h] = vector[h : h + 1, :]
    for h in range(heads):
        @pl.when(me == h * per_head + keeper)
        def _(h=h):
            rvec[me] = vec[h]

        @pl.when(me != h * per_head + keeper)
        def _(h=h):
            block_vector_copy(h, h * per_head + keeper, me).start()

    for c in range(1, chunks):
        local_state(c)
        send_state(c)

    copies[4].wait()
    columns = []
    for h in range(heads):
        scores = scale * lax.dot_general(
            qv[:, h * kd : (h + 1) * kd], kv[:, h * kd : (h + 1) * kd],
            (((1,), (1,)), ((), ())), preferred_element_type=f32,
        )
        masked = jnp.where(rows >= lanes, level[h : h + 1, :], -jnp.inf)
        reach = jnp.max(masked, axis=1, keepdims=True)
        weighted = jnp.exp(masked - reach) * scores
        inner_den = jnp.sum(weighted, axis=1, keepdims=True)
        cumul_col = jnp.sum(
            jnp.where(rows == lanes, cumul[h : h + 1, :], 0.0), axis=1, keepdims=True
        )
        inner[h] = jnp.dot(
            weighted.astype(bf16), vv[:, h * vd : (h + 1) * vd], preferred_element_type=f32
        )
        columns.append((reach, inner_den, cumul_col))

    all_small().wait_recv()

    def widen(out, source):
        for h in range(heads):
            out[h] = jnp.broadcast_to(source[:, h * span : h * span + 1], (ns, 128))

    run_top = jnp.full((1, 128), FLOOR, f32)
    run_dec = jnp.zeros((1, 128), f32)
    for i in range(ns):
        row = rsmall[i]
        top_i = pltpu.roll(row, 64, 1)
        rows_t[i : i + 1, :] = run_top
        rows_d[i : i + 1, :] = run_dec
        early = run_top + row
        joined = jnp.maximum(early, top_i)
        rows_a[i : i + 1, :] = early - joined
        rows_b[i : i + 1, :] = top_i - joined
        run_top = joined
        run_dec = run_dec + row
    lane1 = lax.broadcasted_iota(jnp.int32, (1, 128), 1)
    widen(wide_a, jnp.exp(rows_a[...]))
    widen(wide_b, jnp.exp(rows_b[...]))

    total = jnp.where(lane1 < 64, run_dec, pltpu.roll(run_top, 64, 1))
    gsmall[...] = total
    grsmall[myg] = total

    @pl.loop(myg + 1, ng)
    def _(d):
        group_small_copy(d, myg).start()

    def scan_vector():
        @pl.when(owns_vector)
        def _():
            all_block_vectors().wait_recv()

            run_vec = jnp.zeros((1, 128), f32)
            for i in range(ns):
                nrows[i : i + 1, :] = run_vec
                run_vec = wide_a[myh, i : i + 1, :] * run_vec + wide_b[myh, i : i + 1, :] * rvec[i]
            gvec[...] = run_vec
            grvec[myg] = run_vec

            @pl.loop(myg + 1, ng)
            def _(d):
                group_vector_copy(d, myg).start()

    def scan(c):
        all_state(c).wait_recv()

        for h in range(first[c], first[c + 1]):
            run = jnp.zeros((rp, 128), f32)
            for i in range(ns):
                pbuf[i, h] = run
                run = wide_a[h, i : i + 1, :] * run + wide_b[h, i : i + 1, :] * rbuf[i, h]
            gsend[h] = run
        grecv[myg, first[c] : first[c + 1]] = gsend[first[c] : first[c + 1]]

        @pl.loop(myg + 1, ng)
        def _(d):
            group_copy(c, d, myg).start()

    order = [(what, c) for c in range(chunks) for what in ("scan", "back")]
    order = (
        order[:1] + [("group", 0)] + order[1:2] + [("vector", 0)] + order[2:RET] + [("return", 0)] + order[RET:]
    )

    found = []

    def before_group():
        @pl.loop(0, myg)
        def _(d):
            o = d
            group_small_copy(o, o).wait_recv()

        before_top = jnp.full((1, 128), FLOOR, f32)
        for g in range(ng):
            row = grsmall[g]
            top_g = pltpu.roll(row, 64, 1)
            counts = g < myg
            early = before_top + row
            joined = jnp.maximum(early, top_g)
            a = jnp.where(counts, jnp.exp(early - joined), 1.0)
            b = jnp.where(counts, jnp.exp(top_g - joined), 0.0)
            before_top = jnp.where(counts, joined, before_top)
            group_a[g : g + 1, :] = a
            group_b[g : g + 1, :] = b
        tops = rows_t[...]
        early = before_top + rows_d[...]
        full = jnp.maximum(early, tops)
        rows_t[...] = full
        found.append(rows_t[pl.ds(me, 1), :])
        widen(wide_c, jnp.exp(early - full))
        widen(wide_d, jnp.exp(tops - full))
        for h in range(heads):
            group_wide_a[h] = jnp.broadcast_to(group_a[:, h * span : h * span + 1], (ng, 128))
            group_wide_b[h] = jnp.broadcast_to(group_b[:, h * span : h * span + 1], (ng, 128))

    def return_vector():
        @pl.when(owns_vector)
        def _():
            @pl.loop(0, myg)
            def _(d):
                o = d
                group_vector_copy(o, o).wait_recv()

            before = jnp.zeros((1, 128), f32)
            for g in range(ng):
                before = (
                    group_wide_a[myh, g : g + 1, :] * before
                    + group_wide_b[myh, g : g + 1, :] * grvec[g]
                )
            vectors = wide_c[myh] * before + wide_d[myh] * nrows[...]
            for i in range(ns):
                nback[i] = vectors[i : i + 1, :]
            rnback[myh] = nback[me]

            @pl.loop(1, ns)
            def _(d):
                vector_copy(seq_peer(d), myh).start()

    def back(c):
        @pl.loop(0, myg)
        def _(d):
            o = d
            group_copy(c, o, o).wait_recv()

        for h in range(first[c], first[c + 1]):
            run = jnp.zeros((rp, 128), f32)
            for g in range(ng):
                run = group_wide_a[h, g : g + 1, :] * run + group_wide_b[h, g : g + 1, :] * grecv[g, h]
            for i in range(ns):
                pbuf[i, h] = wide_c[h, i : i + 1, :] * run + wide_d[h, i : i + 1, :] * pbuf[i, h]

        to_columns(lambda o: back_copy(c, o, me).start(), COLUMNS)
        slice_of(pfull, c, me)[...] = pbuf[me, first[c] : first[c + 1]]

    for what, c in order:
        if what == "scan":
            scan(c)
        elif what == "back":
            back(c)
        elif what == "group":
            before_group()
        elif what == "vector":
            scan_vector()
        else:
            return_vector()

    all_small().wait_send()
    for c in range(chunks):
        all_state(c).wait_send()
    for h in range(heads):
        @pl.when(me != h * per_head + keeper)
        def _(h=h):
            block_vector_copy(h, h * per_head + keeper, me).wait_send()

    @pl.when(owns_vector)
    def _():
        @pl.loop(myg + 1, ng)
        def _(d):
            group_vector_copy(d, myg).wait_send()

    @pl.loop(myg + 1, ng)
    def _(d):
        group_small_copy(d, myg).wait_send()
        for c in range(chunks):
            group_copy(c, d, myg).wait_send()

    for h in range(heads):
        @pl.when(me != h * per_head + keeper)
        def _(h=h):
            vector_copy(h * per_head + keeper, h).wait_recv()

    for c in range(chunks):
        all_back(c).wait_recv()

        for h in range(first[c], first[c + 1]):
            reach, inner_den, cumul_col = columns[h]
            query = qv[:, h * kd : (h + 1) * kd]
            carried = scale * jnp.dot(query, pfull[h].astype(bf16), preferred_element_type=f32)
            carried_den = scale * jnp.sum(query.astype(f32) * rnback[h], axis=1, keepdims=True)
            prev = found[0][:, h * span : h * span + 1]
            peak = jnp.maximum(prev, reach)
            inner_factor = jnp.exp(reach - peak)
            outer_factor = jnp.exp(prev - peak)
            denom = inner_factor * inner_den + outer_factor * carried_den
            bound = jnp.maximum(jnp.abs(denom), jnp.exp(-(cumul_col + peak)))
            numer = inner_factor * inner[h] + outer_factor * carried
            o_ref[:, h * vd : (h + 1) * vd] = (numer / bound).astype(bf16)

    for c in range(chunks):
        all_back(c).wait_send()

    @pl.when(owns_vector)
    def _():
        all_vectors().wait_send()


def on_device(ng, ns, queries, key_vectors, value_vectors, input_gate, forget_gate):
    heads, length = input_gate.shape
    kd = queries.shape[1] // heads
    vd = value_vectors.shape[1] // heads
    rp = kd * (vd // 128) // ns
    dma = pltpu.SemaphoreType.DMA

    def wide(*shape):
        return pltpu.VMEM(shape, jnp.float32)

    return pl.pallas_call(
        functools.partial(kernel, ng, ns, heads, kd, vd, length),
        out_shape=pltpu.VMEM(value_vectors.shape, jnp.bfloat16),
        in_specs=[pl.BlockSpec(memory_space=pl.ANY)] * 5,
        out_specs=pl.BlockSpec(memory_space=pltpu.VMEM),
        scratch_shapes=[
            wide(heads, length), wide(heads, length),
            pltpu.VMEM(queries.shape, jnp.bfloat16),
            pltpu.VMEM(key_vectors.shape, jnp.bfloat16),
            pltpu.VMEM(value_vectors.shape, jnp.bfloat16),
            wide(heads, kd, vd), wide(heads, length, vd),
            wide(ns, heads, rp, 128), wide(ns, heads, rp, 128), wide(heads, kd, vd),
            wide(heads, rp, 128), wide(ng, heads, rp, 128),
            wide(1, 128), wide(ns, 1, 128), wide(1, 128), wide(ng, 1, 128),
            wide(heads, 1, 128), wide(ns, 1, 128), wide(1, 128), wide(ng, 1, 128),
            wide(ns, 1, 128), wide(heads, 1, 128), wide(ns, 128),
            wide(ns, 128), wide(ns, 128), wide(ns, 128), wide(ns, 128),
            wide(heads, ns, 128), wide(heads, ns, 128), wide(heads, ns, 128), wide(heads, ns, 128),
            wide(ng, 128), wide(ng, 128), wide(heads, ng, 128), wide(heads, ng, 128),
            dma((5,)),
            dma((len(SIZES),)), dma((len(SIZES),)), dma((1,)), dma((1,)),
            dma((len(SIZES), ng)), dma((len(SIZES), ng)), dma((ng,)), dma((ng,)),
            dma((len(SIZES),)), dma((len(SIZES),)), dma((1,)), dma((heads,)),
            dma((heads,)), dma((1,)), dma((ng,)), dma((ng,)),
        ],
        compiler_params=pltpu.CompilerParams(collective_id=0, has_side_effects=True),
        name="mlstm_layer",
    )(queries, key_vectors, value_vectors, input_gate, forget_gate)


def solution(mesh):
    return jax.shard_map(
        functools.partial(on_device, mesh.shape["grp"], mesh.shape["seq"]),
        mesh=mesh,
        in_specs=(
            P(("grp", "seq"), None),
            P(("grp", "seq"), None),
            P(("grp", "seq"), None),
            P(None, ("grp", "seq")),
            P(None, ("grp", "seq")),
        ),
        out_specs=P(("grp", "seq"), None),
        check_vma=False,
    )
```

```python
import functools

import jax
import jax.numpy as jnp
from jax import lax
from jax.experimental import pallas as pl
from jax.experimental.pallas import tpu as pltpu
from jax.sharding import PartitionSpec as P

MESH = pl.DeviceIdType.MESH
FLOOR = -1e30
SIZES = (1, 1, 1, 1)
RET = 6
COLUMNS = (0, 1, 2, 3, 4, 7, 5, 6)


def split3(x):
    hi = x.astype(jnp.bfloat16)
    rest = x - hi.astype(jnp.float32)
    mid = rest.astype(jnp.bfloat16)
    low = (rest - mid.astype(jnp.float32)).astype(jnp.bfloat16)
    return hi, mid, low


def kernel(
    ng, ns, heads, kd, vd, length,
    q_hbm, k_hbm, v_hbm, ig_hbm, fg_hbm, o_ref,
    ig, fg, qv, kv, vv, state, inner, rbuf, pbuf, pfull, gsend, grecv,
    small, rsmall, gsmall, grsmall, vec, rvec, gvec, grvec, nback, rnback, nrows,
    rows_a, rows_b, rows_t, rows_d, wide_a, wide_b, wide_c, wide_d, group_a, group_b, group_wide_a, group_wide_b,
    in_sem, s1, r1, ss, rs, sg, rg, sgs, rgs, s3, r3, sn, rn, sv, rv, sgv, rgv,
):
    f32, bf16 = jnp.float32, jnp.bfloat16
    chunks = len(SIZES)
    first = [sum(SIZES[:c]) for c in range(chunks + 1)]
    rp = kd * (vd // 128) // ns
    cols = vd // 128
    per_head = ns // heads
    span = 64 // heads
    scale = kd ** (-0.5)
    myg = lax.axis_index("grp")
    me = lax.axis_index("seq")
    myh = me // per_head
    keeper = 0
    owns_vector = (me & (per_head - 1)) == keeper

    def seq_peer(d):
        return (me + d) & (ns - 1)

    def grp_peer(d):
        return (myg + d) & (ng - 1)

    zdim = min(8, ns)
    ydim = ns // zdim
    zbits = zdim.bit_length() - 1
    y, z = me >> zbits, me & (zdim - 1)

    def each_peer(do):
        for d in range(1, ns):
            do(seq_peer(d))

    def far_first(do):
        def far(n, size):
            return min(n, size - n)

        steps = [(dy, dz) for dy in range(ydim) for dz in range(zdim) if dy or dz]
        steps.sort(key=lambda t: (far(t[0], ydim) + far(t[1], zdim)), reverse=True)
        for dy, dz in steps:
            do((((y + dy) & (ydim - 1)) << zbits) | ((z + dz) & (zdim - 1)))

    def to_columns(do, columns):
        for low in range(0, ydim, 2):
            for to in columns:
                for k in range(min(2, ydim)):
                    o = ((low + ((y + k) & (min(2, ydim) - 1))) << zbits) | to
                    pl.when(o != me)(functools.partial(do, o))

    copies = [
        pltpu.make_async_copy(src, dst, in_sem.at[n])
        for n, (src, dst) in enumerate(
            ((fg_hbm, fg), (ig_hbm, ig), (k_hbm, kv), (v_hbm, vv), (q_hbm, qv))
        )
    ]
    for copy in copies:
        copy.start()

    barrier = pltpu.get_barrier_semaphore()

    def greet(device):
        pl.semaphore_signal(barrier, inc=1, device_id=device, device_id_type=MESH)

    each_peer(lambda o: greet((myg, o)))
    for d in range(1, ng):
        greet((grp_peer(d), me))

    zero = jnp.zeros((1, 128), f32)

    @pl.loop(myg + 1, ng)
    def _(g):
        grsmall[g] = zero
        grvec[g] = zero
        for h in range(heads):
            grecv[g, h] = jnp.zeros((rp, 128), f32)

    lane = lax.broadcasted_iota(jnp.int32, (heads, 128), 1)
    head_row = lax.broadcasted_iota(jnp.int32, (heads, 128), 0)
    rows = lax.broadcasted_iota(jnp.int32, (length, length), 0)
    lanes = lax.broadcasted_iota(jnp.int32, (length, length), 1)

    def slice_of(ref, c, o):
        row = pl.multiple_of((o >> (cols.bit_length() - 1)) * rp, 8)
        col = pl.multiple_of((o & (cols - 1)) * 128, 128)
        return ref.at[pl.ds(first[c], SIZES[c]), pl.ds(row, rp), pl.ds(col, 128)]

    def part(c):
        return pl.ds(first[c], SIZES[c])

    def remote(src, dst, send, recv, device):
        return pltpu.make_async_remote_copy(
            src_ref=src, dst_ref=dst, send_sem=send, recv_sem=recv, device_id=device, device_id_type=MESH
        )

    def small_copy(o, slot):
        return remote(
            small, rsmall.at[slot], ss.at[0], rs.at[0], (myg, o)
        )

    def block_vector_copy(h, o, slot):
        return remote(vec.at[h], rvec.at[slot], sv.at[h], rv.at[0], (myg, o))

    def group_vector_copy(o, slot):
        return remote(gvec, grvec.at[slot], sgv.at[o], rgv.at[slot], (o, me))

    def state_copy(c, o, slot):
        return remote(
            slice_of(state, c, o), rbuf.at[slot, part(c)], s1.at[c], r1.at[c], (myg, o)
        )

    def back_copy(c, o, slot):
        return remote(
            pbuf.at[o, part(c)], slice_of(pfull, c, slot), s3.at[c], r3.at[c], (myg, o)
        )

    def vector_copy(o, h):
        return remote(nback.at[o], rnback.at[h], sn.at[0], rn.at[h], (myg, o))

    others = pl.ds(0, ns - 1)

    def all_small():
        return remote(rsmall.at[others], rsmall.at[others], ss.at[0], rs.at[0], (myg, me))

    def all_state(c):
        ref = rbuf.at[others, part(c)]
        return remote(ref, ref, s1.at[c], r1.at[c], (myg, me))

    def all_back(c):
        ref = pbuf.at[others, part(c)]
        return remote(ref, ref, s3.at[c], r3.at[c], (myg, me))

    def all_block_vectors():
        return remote(rvec.at[others], rvec.at[others], sv.at[0], rv.at[0], (myg, me))

    def all_vectors():
        return remote(nback.at[others], nback.at[others], sn.at[0], rn.at[0], (myg, me))

    def group_small_copy(o, slot):
        return remote(gsmall, grsmall.at[slot], sgs.at[o], rgs.at[slot], (o, me))

    def group_copy(c, o, slot):
        return remote(
            gsend.at[part(c)], grecv.at[slot, part(c)], sg.at[c, o], rg.at[c, slot], (o, me)
        )

    upper = jnp.where(rows <= lanes, 1.0, 0.0).astype(bf16)
    copies[0].wait()
    copies[1].wait()
    forget = fg[...]
    logf = jnp.minimum(forget, 0.0) - jnp.log1p(jnp.exp(-jnp.abs(forget)))

    def exact_rows(values, matrix):
        hi, mid, low = split3(values)
        lhs = jnp.concatenate([hi, mid, low, jnp.zeros_like(low)], axis=0)
        out = jnp.dot(lhs, matrix, preferred_element_type=f32)
        n = values.shape[0]
        return out[0:n] + out[n : 2 * n] + out[2 * n : 3 * n]

    cumul = exact_rows(logf, upper)
    level = ig[...] - cumul
    decay = cumul[:, length - 1 : length]
    level_top = jnp.max(level, axis=1, keepdims=True)
    weight = jnp.exp(level - level_top)
    top = decay + level_top

    mine = jnp.where(lane < 64, decay, top)
    pick = lax.div(lax.rem(lane, 64), span) == head_row
    scalars = jnp.sum(jnp.where(pick, mine, 0.0), axis=0, keepdims=True)

    copies[2].wait()
    copies[3].wait()

    def local_state(c):
        for h in range(first[c], first[c + 1]):
            turned = kv[:, h * kd : (h + 1) * kd].astype(f32).T
            scaled = (turned * weight[h : h + 1, :]).astype(bf16)
            state[h] = jnp.dot(scaled, vv[:, h * vd : (h + 1) * vd], preferred_element_type=f32)
        rbuf[me, first[c] : first[c + 1]] = slice_of(state, c, me)[...]

    def send_state(c):
        far_first(lambda o: state_copy(c, o, me).start())

    small[...] = scalars
    rsmall[me] = scalars
    for c in range(chunks):
        local_state(c)
    pl.semaphore_wait(barrier, ns - 1 + ng - 1)

    each_peer(lambda o: small_copy(o, me).start())

    send_state(0)
    for h in range(heads):
        vector = exact_rows(weight, kv[:, h * kd : (h + 1) * kd])
        vec[h] = vector[h : h + 1, :]
    for h in range(heads):
        @pl.when(me == h * per_head + keeper)
        def _(h=h):
            rvec[me] = vec[h]

        @pl.when(me != h * per_head + keeper)
        def _(h=h):
            block_vector_copy(h, h * per_head + keeper, me).start()

    for c in range(1, chunks):
        send_state(c)

    copies[4].wait()
    columns = []
    for h in range(heads):
        scores = scale * lax.dot_general(
            qv[:, h * kd : (h + 1) * kd], kv[:, h * kd : (h + 1) * kd],
            (((1,), (1,)), ((), ())), preferred_element_type=f32,
        )
        masked = jnp.where(rows >= lanes, level[h : h + 1, :], -jnp.inf)
        reach = jnp.max(masked, axis=1, keepdims=True)
        weighted = jnp.exp(masked - reach) * scores
        inner_den = jnp.sum(weighted, axis=1, keepdims=True)
        cumul_col = jnp.sum(
            jnp.where(rows == lanes, cumul[h : h + 1, :], 0.0), axis=1, keepdims=True
        )
        inner[h] = jnp.dot(
            weighted.astype(bf16), vv[:, h * vd : (h + 1) * vd], preferred_element_type=f32
        )
        columns.append((reach, inner_den, cumul_col))

    all_small().wait_recv()

    def widen(out, source):
        for h in range(heads):
            out[h] = jnp.broadcast_to(source[:, h * span : h * span + 1], (ns, 128))

    run_top = jnp.full((1, 128), FLOOR, f32)
    run_dec = jnp.zeros((1, 128), f32)
    for i in range(ns):
        row = rsmall[i]
        top_i = pltpu.roll(row, 64, 1)
        rows_t[i : i + 1, :] = run_top
        rows_d[i : i + 1, :] = run_dec
        early = run_top + row
        joined = jnp.maximum(early, top_i)
        rows_a[i : i + 1, :] = early - joined
        rows_b[i : i + 1, :] = top_i - joined
        run_top = joined
        run_dec = run_dec + row
    lane1 = lax.broadcasted_iota(jnp.int32, (1, 128), 1)
    widen(wide_a, jnp.exp(rows_a[...]))
    widen(wide_b, jnp.exp(rows_b[...]))

    total = jnp.where(lane1 < 64, run_dec, pltpu.roll(run_top, 64, 1))
    gsmall[...] = total
    grsmall[myg] = total

    @pl.loop(myg + 1, ng)
    def _(d):
        group_small_copy(d, myg).start()

    def scan_vector():
        @pl.when(owns_vector)
        def _():
            all_block_vectors().wait_recv()

            run_vec = jnp.zeros((1, 128), f32)
            for i in range(ns):
                nrows[i : i + 1, :] = run_vec
                run_vec = wide_a[myh, i : i + 1, :] * run_vec + wide_b[myh, i : i + 1, :] * rvec[i]
            gvec[...] = run_vec
            grvec[myg] = run_vec

            @pl.loop(myg + 1, ng)
            def _(d):
                group_vector_copy(d, myg).start()

    def scan(c):
        all_state(c).wait_recv()

        for h in range(first[c], first[c + 1]):
            run = jnp.zeros((rp, 128), f32)
            for i in range(ns):
                pbuf[i, h] = run
                run = wide_a[h, i : i + 1, :] * run + wide_b[h, i : i + 1, :] * rbuf[i, h]
            gsend[h] = run
        grecv[myg, first[c] : first[c + 1]] = gsend[first[c] : first[c + 1]]

        @pl.loop(myg + 1, ng)
        def _(d):
            group_copy(c, d, myg).start()

    order = [(what, c) for c in range(chunks) for what in ("scan", "back")]
    order = (
        order[:1] + [("group", 0)] + order[1:2] + [("vector", 0)] + order[2:RET] + [("return", 0)] + order[RET:]
    )

    found = []

    def before_group():
        @pl.loop(0, myg)
        def _(d):
            o = d
            group_small_copy(o, o).wait_recv()

        before_top = jnp.full((1, 128), FLOOR, f32)
        for g in range(ng):
            row = grsmall[g]
            top_g = pltpu.roll(row, 64, 1)
            counts = g < myg
            early = before_top + row
            joined = jnp.maximum(early, top_g)
            a = jnp.where(counts, jnp.exp(early - joined), 1.0)
            b = jnp.where(counts, jnp.exp(top_g - joined), 0.0)
            before_top = jnp.where(counts, joined, before_top)
            group_a[g : g + 1, :] = a
            group_b[g : g + 1, :] = b
        tops = rows_t[...]
        early = before_top + rows_d[...]
        full = jnp.maximum(early, tops)
        rows_t[...] = full
        found.append(rows_t[pl.ds(me, 1), :])
        widen(wide_c, jnp.exp(early - full))
        widen(wide_d, jnp.exp(tops - full))
        for h in range(heads):
            group_wide_a[h] = jnp.broadcast_to(group_a[:, h * span : h * span + 1], (ng, 128))
            group_wide_b[h] = jnp.broadcast_to(group_b[:, h * span : h * span + 1], (ng, 128))

    def return_vector():
        @pl.when(owns_vector)
        def _():
            @pl.loop(0, myg)
            def _(d):
                o = d
                group_vector_copy(o, o).wait_recv()

            before = jnp.zeros((1, 128), f32)
            for g in range(ng):
                before = (
                    group_wide_a[myh, g : g + 1, :] * before
                    + group_wide_b[myh, g : g + 1, :] * grvec[g]
                )
            vectors = wide_c[myh] * before + wide_d[myh] * nrows[...]
            for i in range(ns):
                nback[i] = vectors[i : i + 1, :]
            rnback[myh] = nback[me]

            @pl.loop(1, ns)
            def _(d):
                vector_copy(seq_peer(d), myh).start()

    def back(c):
        @pl.loop(0, myg)
        def _(d):
            o = d
            group_copy(c, o, o).wait_recv()

        for h in range(first[c], first[c + 1]):
            run = jnp.zeros((rp, 128), f32)
            for g in range(ng):
                run = group_wide_a[h, g : g + 1, :] * run + group_wide_b[h, g : g + 1, :] * grecv[g, h]
            for i in range(ns):
                pbuf[i, h] = wide_c[h, i : i + 1, :] * run + wide_d[h, i : i + 1, :] * pbuf[i, h]

        to_columns(lambda o: back_copy(c, o, me).start(), COLUMNS)
        slice_of(pfull, c, me)[...] = pbuf[me, first[c] : first[c + 1]]

    for what, c in order:
        if what == "scan":
            scan(c)
        elif what == "back":
            back(c)
        elif what == "group":
            before_group()
        elif what == "vector":
            scan_vector()
        else:
            return_vector()

    all_small().wait_send()
    for c in range(chunks):
        all_state(c).wait_send()
    for h in range(heads):
        @pl.when(me != h * per_head + keeper)
        def _(h=h):
            block_vector_copy(h, h * per_head + keeper, me).wait_send()

    @pl.when(owns_vector)
    def _():
        @pl.loop(myg + 1, ng)
        def _(d):
            group_vector_copy(d, myg).wait_send()

    @pl.loop(myg + 1, ng)
    def _(d):
        group_small_copy(d, myg).wait_send()
        for c in range(chunks):
            group_copy(c, d, myg).wait_send()

    for h in range(heads):
        @pl.when(me != h * per_head + keeper)
        def _(h=h):
            vector_copy(h * per_head + keeper, h).wait_recv()

    for c in range(chunks):
        all_back(c).wait_recv()

        for h in range(first[c], first[c + 1]):
            reach, inner_den, cumul_col = columns[h]
            query = qv[:, h * kd : (h + 1) * kd]
            carried = scale * jnp.dot(query, pfull[h].astype(bf16), preferred_element_type=f32)
            carried_den = scale * jnp.sum(query.astype(f32) * rnback[h], axis=1, keepdims=True)
            prev = found[0][:, h * span : h * span + 1]
            peak = jnp.maximum(prev, reach)
            inner_factor = jnp.exp(reach - peak)
            outer_factor = jnp.exp(prev - peak)
            denom = inner_factor * inner_den + outer_factor * carried_den
            bound = jnp.maximum(jnp.abs(denom), jnp.exp(-(cumul_col + peak)))
            numer = inner_factor * inner[h] + outer_factor * carried
            o_ref[:, h * vd : (h + 1) * vd] = (numer / bound).astype(bf16)

    for c in range(chunks):
        all_back(c).wait_send()

    @pl.when(owns_vector)
    def _():
        all_vectors().wait_send()


def on_device(ng, ns, queries, key_vectors, value_vectors, input_gate, forget_gate):
    heads, length = input_gate.shape
    kd = queries.shape[1] // heads
    vd = value_vectors.shape[1] // heads
    rp = kd * (vd // 128) // ns
    dma = pltpu.SemaphoreType.DMA

    def wide(*shape):
        return pltpu.VMEM(shape, jnp.float32)

    return pl.pallas_call(
        functools.partial(kernel, ng, ns, heads, kd, vd, length),
        out_shape=pltpu.VMEM(value_vectors.shape, jnp.bfloat16),
        in_specs=[pl.BlockSpec(memory_space=pl.ANY)] * 5,
        out_specs=pl.BlockSpec(memory_space=pltpu.VMEM),
        scratch_shapes=[
            wide(heads, length), wide(heads, length),
            pltpu.VMEM(queries.shape, jnp.bfloat16),
            pltpu.VMEM(key_vectors.shape, jnp.bfloat16),
            pltpu.VMEM(value_vectors.shape, jnp.bfloat16),
            wide(heads, kd, vd), wide(heads, length, vd),
            wide(ns, heads, rp, 128), wide(ns, heads, rp, 128), wide(heads, kd, vd),
            wide(heads, rp, 128), wide(ng, heads, rp, 128),
            wide(1, 128), wide(ns, 1, 128), wide(1, 128), wide(ng, 1, 128),
            wide(heads, 1, 128), wide(ns, 1, 128), wide(1, 128), wide(ng, 1, 128),
            wide(ns, 1, 128), wide(heads, 1, 128), wide(ns, 128),
            wide(ns, 128), wide(ns, 128), wide(ns, 128), wide(ns, 128),
            wide(heads, ns, 128), wide(heads, ns, 128), wide(heads, ns, 128), wide(heads, ns, 128),
            wide(ng, 128), wide(ng, 128), wide(heads, ng, 128), wide(heads, ng, 128),
            dma((5,)),
            dma((len(SIZES),)), dma((len(SIZES),)), dma((1,)), dma((1,)),
            dma((len(SIZES), ng)), dma((len(SIZES), ng)), dma((ng,)), dma((ng,)),
            dma((len(SIZES),)), dma((len(SIZES),)), dma((1,)), dma((heads,)),
            dma((heads,)), dma((1,)), dma((ng,)), dma((ng,)),
        ],
        compiler_params=pltpu.CompilerParams(collective_id=0, has_side_effects=True),
        name="mlstm_layer",
    )(queries, key_vectors, value_vectors, input_gate, forget_gate)


def solution(mesh):
    return jax.shard_map(
        functools.partial(on_device, mesh.shape["grp"], mesh.shape["seq"]),
        mesh=mesh,
        in_specs=(
            P(("grp", "seq"), None),
            P(("grp", "seq"), None),
            P(("grp", "seq"), None),
            P(None, ("grp", "seq")),
            P(None, ("grp", "seq")),
        ),
        out_specs=P(("grp", "seq"), None),
        check_vma=False,
    )
```
